512 devices in a mesh: prow: 16 (over y_hi, x, core), pcol: 32 (over y_lo, z).
Axes of the slice: x: 4, y: 4 (y_hi: 2, y_lo: 2; y = y_hi * 2 + y_lo), z: 16, core: 2. Of those that a mesh axis runs over, the one named last changes fastest.
Arguments:
- sep_inverse: bfloat16 [2, 16, 256, 1, 32, 256], P(None, 'prow', None, None, 'pcol'), may hold values from -2 to 30, as said below
- panels: bfloat16 [4, 2, 16, 256, 256], P(None, None, 'prow', 'pcol'), may hold values from -0.0625 to 0.0625
- ancestors: int32 [4, 32], replicated, may hold values from 0 to 1, as said below
- window_factor: bfloat16 [6, 256, 256], replicated, may hold values from -0.1875 to 0.1875
- diag_inverse: bfloat16 [4, 256, 256], replicated, may hold values from -1 to 4, as said below
Outputs:
- ys: float32 [4, 2, 16, 256, 256], P(None, None, 'prow', 'pcol')
- window_inverse: float32 [1024, 1024], P('prow', 'pcol')
The draws below stay inside these ranges and needn't reach their ends.
Inputs may be any that keep to these rules, and one draw needn't show every extreme that they name: sep_inverse read as in the first step is symmetric. `diag_inverse`: each block is symmetric. ancestors[k + 1, t] <= ancestors[k, t]: a supernode's ancestor tiles lie among those of the one before it.
All inputs are finite; a program needn't handle non-finite values.
Results may differ from the reference program's by a relative error of at most 0.00035.
Values may be sent and summed in bfloat16 or wider, within the bound.
A program may use at most 64 MiB of HBM per device.

```python
import math
import jax
import jax.numpy as jnp
from jax import lax

W = 256
KS = 4
RC = 2
NT = 32
CC = 1
SEP = 8192
PAIRS = 6
N_PROW = 16
N_PCOL = 32


def noise(key, shape):
    return jnp.clip(jax.random.normal(key, shape, jnp.float32), -4.0, 4.0)


def draw_sep_inverse(key, part):
    off_scale = 0.35 / math.sqrt(SEP * 2.0)
    lower_end, upper_end = (0.5, 1.5)

    def one_row(tile_row):

        def one_tile(tile_column):
            forward = noise(jax.random.fold_in(key, tile_row * NT + tile_column), (W, W))
            backward = noise(jax.random.fold_in(key, tile_column * NT + tile_row), (W, W))
            return (forward + backward.T) * off_scale
        row_tiles = jax.vmap(one_tile)(jnp.arange(NT, dtype=jnp.int32))
        diagonal_terms = jax.random.uniform(jax.random.fold_in(key, NT * NT + tile_row), (W,), jnp.float32, lower_end, upper_end)
        on_diagonal = (jnp.arange(NT, dtype=jnp.int32) == tile_row).astype(jnp.float32)[:, None, None]
        row_tiles = row_tiles + on_diagonal * jnp.diag(diagonal_terms)[None]
        return (16.0 * jnp.transpose(row_tiles, (1, 0, 2))).reshape(W, SEP).astype(jnp.bfloat16)
    row_blocks = lax.map(one_row, jnp.arange(NT, dtype=jnp.int32))
    return row_blocks.reshape(RC, N_PROW, W, CC, N_PCOL, W)


def draw_diag_inverse(key, part):
    raw_noise = noise(jax.random.fold_in(key, 7), (KS, W, W))
    identity = jnp.eye(W, dtype=jnp.float32)
    off_part = (raw_noise + jnp.transpose(raw_noise, (0, 2, 1))) * (0.6 / math.sqrt(2.0 * W)) * (1.0 - identity)[None]
    diagonal_terms = jax.random.uniform(jax.random.fold_in(key, 11), (KS, W), jnp.float32, 1.0, 3.0)
    return (off_part + identity[None] * diagonal_terms[:, None, :]).astype(jnp.bfloat16)


def draw_ancestors(key, part):
    levels = jax.random.randint(jax.random.fold_in(key, 3), (NT,), 0, KS + 2)
    return (levels[None, :] > jnp.arange(KS, dtype=jnp.int32)[:, None]).astype(jnp.int32)


def steps_of(own_key, dims, pieces, low, top_value):
    gain = 1.0
    for axis_at, parts in pieces:
        steps = jax.random.uniform(jax.random.fold_in(jax.random.fold_in(own_key, 6), axis_at), (parts,), jnp.float32, low / len(pieces), top_value / len(pieces))
        gain = gain * jnp.repeat(jnp.exp(steps), dims[axis_at] // parts).reshape((-1,) + (1,) * (len(dims) - 1 - axis_at))
    return gain


def normal_values(key, dims, width, most, cuts=(), kind=jnp.bfloat16):
    values = jax.random.normal(key, dims, jnp.float32) * width
    if len(cuts) > 0:
        values = steps_of(key, dims, cuts, -0.22, 0.18) * values
    return jnp.clip(values, min=-most, max=most).astype(kind)


def setup_inputs(seed: int = 0) -> dict:
    streams_of = jax.random.split(jax.random.key(seed), 6)
    return {
        "sep_inverse": draw_sep_inverse(jax.random.fold_in(streams_of[5], 71), 0),
        "panels": normal_values(streams_of[1], (KS, RC, N_PROW, W, W), SEP ** -0.5, 0.0625, ((2, 16), (3, 32))),
        "ancestors": draw_ancestors(jax.random.fold_in(streams_of[5], 71), 0),
        "window_factor": normal_values(streams_of[3], (PAIRS, W, W), (KS * W) ** -0.5, 0.1875),
        "diag_inverse": draw_diag_inverse(jax.random.fold_in(streams_of[5], 71), 0),
    }


def product(operand_left, operand_right):
    return jnp.dot(operand_left, operand_right, precision=lax.Precision.HIGHEST, preferred_element_type=jnp.float32)


def pair_index(earlier, later):
    return later * (later - 1) // 2 + earlier


def window_step(later, window_sums, window_factor, diag_inverse, window_blocks):
    coupled = []
    for earlier in range(later):
        running = window_sums[earlier]
        for partner in range(later):
            running = running + product(window_blocks[(earlier, partner)], window_factor[pair_index(partner, later)].astype(jnp.float32))
        upper_block = -running
        window_blocks[(earlier, later)] = upper_block
        window_blocks[(later, earlier)] = upper_block.T
        coupled.append(upper_block)
    running = window_sums[later]
    for earlier in range(later):
        running = running + product(window_factor[pair_index(earlier, later)].astype(jnp.float32).T, coupled[earlier])
    window_blocks[(later, later)] = diag_inverse[later].astype(jnp.float32) - running


def assemble_window(window_blocks, supernodes):
    return jnp.block([[window_blocks[(first, second)] for second in range(supernodes)] for first in range(supernodes)])


def reference(sep_inverse, panels, ancestors, window_factor, diag_inverse):
    sep_columns = sep_inverse.reshape(SEP, CC, N_PCOL, W)
    window_blocks = {}
    columns = []
    for later in range(KS):
        row_keep = jnp.repeat(ancestors[later], W, total_repeat_length=SEP)
        factor = panels[later].reshape(SEP, W) * row_keep[:, None].astype(jnp.bfloat16)
        grouped = factor.reshape(CC, N_PCOL, W, W)

        def add_group(running_sum, column_group, grouped=grouped):
            sep_piece = lax.dynamic_index_in_dim(sep_columns, column_group, 2, keepdims=False).reshape(SEP, CC * W)
            factor_piece = lax.dynamic_index_in_dim(grouped, column_group, 1, keepdims=False).reshape(CC * W, W)
            partial_value = jnp.dot(sep_piece, factor_piece, preferred_element_type=jnp.float32)
            return running_sum + partial_value, None

        summed, _ = lax.scan(add_group, jnp.zeros((SEP, W), jnp.float32), jnp.arange(N_PCOL, dtype=jnp.int32))
        carried = -summed
        for earlier in range(later):
            carried = carried - product(columns[earlier], window_factor[pair_index(earlier, later)].astype(jnp.float32))
        current = carried * row_keep[:, None].astype(jnp.float32)
        factor_wide = factor.astype(jnp.float32)
        window_parts = [product(columns[earlier].T, factor_wide) for earlier in range(later)]
        window_parts.append(product(factor_wide.T, current))
        window_step(later, window_parts, window_factor, diag_inverse, window_blocks)
        columns.append(current)
    ys = jnp.stack(columns).reshape(KS, RC, N_PROW, W, W)
    return ys, assemble_window(window_blocks, KS)
```

```python
import jax
import jax.numpy as jnp
from jax import lax
from jax.experimental import pallas as pl
from jax.experimental.pallas import tpu as pltpu
from jax.sharding import PartitionSpec as P

MESH = pl.DeviceIdType.MESH
F32 = jnp.float32
BF16 = jnp.bfloat16
NP = 16
NZ = 16
W = 256
KS = 4
NC = KS * W


def rem(value, n):
    return lax.rem(value, jnp.int32(n))


def div(value, n):
    return lax.div(value, jnp.int32(n))


def dot(left, right):
    return jnp.dot(left, right, preferred_element_type=F32)


def dot_rows(left, right):
    return lax.dot_general(left, right, (((0,), (0,)), ((), ())), preferred_element_type=F32)


def halves(value):
    high = value.astype(BF16)
    low = (value - high.astype(F32)).astype(BF16)
    return high, low


def pair_index(earlier, later):
    return later * (later - 1) // 2 + earlier


def drain(ref, sem):
    pltpu.make_async_copy(ref, ref, sem).wait()


def kernel(
    s_ref, p_ref, anc_ref, l_ref, d_ref, y_ref, v_ref,
    fg, wide, st, give, keep, pairb, red, mh, ml, uh, ul, ysend, yrecv, vsend, vrecv, wc, dm, dmw, vps, vpr,
    ag_send, ag_recv, ye_send, ye_recv, pair_send, pair_recv, red_send, red_recv,
    y_send, y_recv, v_send, v_recv, f_send, f_recv,
):
    p = lax.axis_index("prow")
    q = lax.axis_index("pcol")
    core = rem(p, 2)
    chip = div(p, 2)
    ylo = div(q, NZ)
    z = rem(q, NZ)

    def copy(src, dst, send, recv, prow, pcol):
        return pltpu.make_async_remote_copy(
            src_ref=src, dst_ref=dst, send_sem=send, recv_sem=recv,
            device_id=(prow, pcol), device_id_type=MESH,
        )

    barrier = pltpu.get_barrier_semaphore()
    right = rem(z + 1, NZ)
    left = rem(z + NZ - 1, NZ)
    for dp in range(NP):
        for dy in range(2):
            if dp or dy:
                pl.semaphore_signal(
                    barrier, inc=1,
                    device_id=(rem(p + dp, NP), rem(ylo + dy, 2) * NZ + z), device_id_type=MESH,
                )
    for other in (right, left):
        pl.semaphore_signal(barrier, inc=1, device_id=(p, ylo * NZ + other), device_id_type=MESH)

    rows = []
    for r in range(2):
        parts = []
        for k in range(KS):
            flag = anc_ref[k, r * NP + p].astype(F32)
            parts.append(p_ref[k, r].astype(F32) * flag)
        rows.append(jnp.concatenate(parts, axis=1))
    fg[z, ylo] = jnp.concatenate(rows, axis=0).astype(BF16)

    pl.semaphore_wait(barrier, 33)

    ycopy = copy(fg.at[z, ylo], fg.at[z, ylo], ye_send, ye_recv, p, (1 - ylo) * NZ + z)

    def ring(way, e, step):
        row = rem(ylo + e, 2)
        at = rem(z + NZ - step, NZ) if way == 0 else rem(z + step, NZ)
        to = right if way == 0 else left
        return copy(
            fg.at[at, row], fg.at[at, row], ag_send.at[way, e, step], ag_recv.at[way, e, step],
            p, ylo * NZ + to,
        )

    def task_s(r):
        def run():
            value = s_ref[r].astype(F32).reshape(2, NZ, 8, W)
            for y in range(2):
                wide[:, y, r] = value[y]

        return run

    def task_t():
        st[...] = wide[...].reshape(512, W).T.astype(BF16)

    def put(m, k, value):
        high, low = halves(value)
        mh[m, :, k * W : (k + 1) * W] = high
        ml[m, :, k * W : (k + 1) * W] = low

    def times(m, k, later):
        both = jnp.concatenate(
            [mh[m, :, k * W : (k + 1) * W], ml[m, :, k * W : (k + 1) * W]], axis=0
        )
        out = dot(both, l_ref[pair_index(k, later)])
        return out[:W] + out[W:]

    def coupling(m, k):
        return l_ref[pair_index(m, k)].astype(F32)

    def task_zero():
        rows_at = lax.broadcasted_iota(jnp.int32, (W, W), 0)
        cols_at = lax.broadcasted_iota(jnp.int32, (W, W), 1)
        eye = jnp.where(rows_at == cols_at, 1.0, 0.0).astype(BF16)
        zero = jnp.zeros((W, W), BF16)
        for m in range(KS):
            for k in range(m + 1):
                mh[m, :, k * W : (k + 1) * W] = eye if m == k else zero
                ml[m, :, k * W : (k + 1) * W] = zero
        for m in range(KS - 1):
            put(m, m + 1, -coupling(m, m + 1))

    def task_m2():
        for m in range(2):
            put(m, m + 2, -(coupling(m, m + 2) + times(m, m + 1, m + 2)))

    def task_m3():
        put(0, 3, -(coupling(0, 3) + times(0, 1, 3) + times(0, 2, 3)))

    share = ylo * NP + p
    block = div(share, 8)
    first = pl.multiple_of(rem(share, 8) * 32, 32)
    lane = lax.broadcasted_iota(jnp.int32, (32, 128), 1)

    def task_d():
        dd = d_ref[block, pl.ds(first, 32), :]
        for a in range(8):
            cols = slice(128 * a, 128 * a + 128)
            dm[a] = dot(dd, mh[block, :, cols]) + dot(dd, ml[block, :, cols])
        group = div(z, 4)
        sub = rem(z, 4)
        low_cols = dm[group]
        high_cols = dm[4 + group]
        picked = jnp.zeros((32, 128), F32)
        for b in range(4):
            one = jnp.where(
                lane < 32,
                pltpu.roll(low_cols, (128 - 32 * b) % 128, 1),
                pltpu.roll(high_cols, (160 - 32 * b) % 128, 1),
            )
            picked = jnp.where(sub == b, one, picked)
        picked = jnp.where(lane < 64, picked, 0.0)
        high = picked.astype(BF16).astype(F32)
        dmw[...] = jnp.where(lane < 64, high, pltpu.roll(picked - high, 64, 1)).astype(BF16)

    def task_wc():
        wc[...] = jnp.zeros(wc.shape, F32)

    tasks = [task_s(0), task_s(1), task_t, task_zero, task_m2, task_m3, task_d, task_wc]

    ycopy.start()
    for way in range(2):
        ring(way, 0, 0).start()
    tasks.pop(0)()
    ycopy.wait_recv()
    for way in range(2):
        ring(way, 1, 0).start()
    last = (8, 7)
    for step in range(1, 9):
        if tasks:
            tasks.pop(0)()
        for e in range(2):
            for way in range(2):
                if step <= last[way]:
                    ring(way, e, step - 1).wait_recv()
                    if step < last[way]:
                        ring(way, e, step).start()
    while tasks:
        tasks.pop(0)()

    def gathered(k):
        return fg[:, :, :, k * W : (k + 1) * W].reshape(512, W)

    mine = pl.multiple_of(core * 128, 128)
    theirs = pl.multiple_of((1 - core) * 128, 128)
    mate = p + 1 - 2 * core

    def pair(k):
        return copy(give.at[k], pairb.at[k], pair_send.at[k], pair_recv.at[k], mate, q)

    def spread(k, d):
        to = rem(chip + d, 8)
        rows_to = pl.multiple_of(to * 16, 16)
        return copy(
            keep.at[k, pl.ds(rows_to, 16)], red.at[k, d - 1], red_send.at[k], red_recv.at[k],
            to * 2 + core, q,
        )

    for k in range(KS):
        give[k] = dot(st[pl.ds(theirs, 128), :], gathered(k))
        keep[k] = dot(st[pl.ds(mine, 128), :], gathered(k))
        pair(k).start()
    for k in range(KS):
        pair(k).wait_recv()
        keep[k] = keep[k] + pairb[k]
        for d in range(1, 8):
            spread(k, d).start()

    for k in range(KS):
        if k == 0:
            uh[0] = gathered(0)
            ul[0] = jnp.zeros((512, W), BF16)
        else:
            total = gathered(k).astype(F32)
            for m in range(k):
                left_side = gathered(m)
                cols = slice(k * W, (k + 1) * W)
                total = total + dot(left_side, mh[m, :, cols]) + dot(left_side, ml[m, :, cols])
            high, low = halves(total)
            uh[k] = high
            ul[k] = low

    own_rows = pl.multiple_of(chip * 16, 16)
    blocks = []
    for k in range(KS):
        drain(red.at[k], red_recv.at[k])
        total = keep[k, pl.ds(own_rows, 16), :]
        for d in range(7):
            total = total + red[k, d]
        for m in range(k):
            high, low = halves(blocks[m])
            both = dot(jnp.concatenate([high, low], axis=0), l_ref[pair_index(m, k)])
            total = total - (both[:16] + both[16:])
        blocks.append(total)
        for e in range(2):
            ysend[e, :, k * W : (k + 1) * W] = total[8 * e : 8 * e + 8]

    lane8 = lax.broadcasted_iota(jnp.int32, (8, 128), 1)
    for a in range(4):
        k, at = divmod(128 * a, W)
        first_a = blocks[k][:, at : at + 128]
        second_a = blocks[k + 2][:, at : at + 128]
        for b in range(4):
            def moved(value, group):
                shift = (32 * (group - b)) % 128
                return pltpu.roll(value, shift, 1) if shift else value

            piece = jnp.where(
                lane8 < 64,
                jnp.where(lane8 < 32, moved(first_a[:8], 0), moved(second_a[:8], 1)),
                jnp.where(lane8 < 96, moved(first_a[8:], 2), moved(second_a[8:], 3)),
            )
            vsend[4 * a + b] = piece

    chunk = core * 8 + chip
    here = z == p

    def ypart(e):
        to = 2 * chunk + e
        return copy(ysend.at[e], yrecv.at[ylo], y_send.at[e], y_recv.at[ylo], z, to)

    def ylocal(e):
        return pltpu.make_async_copy(ysend.at[e], yrecv.at[ylo], y_recv.at[ylo])

    def vpart(d):
        to = rem(z + d, NZ)
        return copy(
            vsend.at[to], vrecv.at[chunk], v_send.at[min(d, 1)], v_recv, z, ylo * NZ + to,
        )

    def vlocal():
        return pltpu.make_async_copy(vsend.at[z], vrecv.at[chunk], v_recv)

    for d in range(1, NZ):
        vpart(d).start()

    @pl.when(here)
    def _():
        vlocal().start()

    @pl.when(jnp.logical_not(here))
    def _():
        vpart(0).start()

    for e in range(2):
        home = jnp.logical_and(here, q == 2 * chunk + e)

        @pl.when(home)
        def _():
            ylocal(e).start()

        @pl.when(jnp.logical_not(home))
        def _():
            ypart(e).start()

    drain(vrecv, v_recv)
    got = vrecv[...].reshape(2, 8, 8, 128)
    wide_lane = lax.broadcasted_iota(jnp.int32, (8, 8, 128), 2)
    for y in range(2):
        for h in range(2):
            value = got[y]
            if h:
                value = pltpu.roll(value, 64, 2)
            value = jnp.where(wide_lane < 64, value, 0.0)
            high = value.astype(BF16).astype(F32)
            value = jnp.where(wide_lane < 64, high, pltpu.roll(value - high, 64, 2))
            for n in range(8):
                wc[2 * n + h, y, ylo] = value[n]
    columns = wc[...].reshape(512, 128).astype(BF16)
    lane16 = lax.broadcasted_iota(jnp.int32, (4, 16, 128), 2)
    for k in range(KS):
        cols = slice(k * W, (k + 1) * W)
        total = dot_rows(uh[k], columns) + dot_rows(ul[k], columns)
        total = total + dot_rows(mh[block, pl.ds(first, 32), cols], dmw[...])
        total = total + dot_rows(ml[block, pl.ds(first, 32), cols], dmw[...])
        total = total + pltpu.roll(total, 64, 1)
        total = total.reshape(4, 4, 16, 128)
        for e in range(2):
            packed = None
            for g in range(4):
                shift = (32 * (g - e)) % 128
                value = total[:, g]
                if shift:
                    value = pltpu.roll(value, shift, 2)
                packed = value if packed is None else jnp.where(lane16 < 32 * g, packed, value)
            vps[4 * k : 4 * k + 4, e] = packed

    def final(dp, dy):
        to = rem(p + dp, NP)
        row = rem(ylo + dy, 2)
        return copy(
            vps.at[to, row], vpr.at[2 * dp + dy - 1], f_send, f_recv, to, row * NZ + z
        )

    for dp in range(NP):
        for dy in range(2):
            if dp or dy:
                final(dp, dy).start()

    for r in range(2):
        drain(yrecv.at[r], y_recv.at[r])
        for k in range(KS):
            flag = anc_ref[k, r * NP + p].astype(F32)
            y_ref[k, r] = yrecv[r, :, k * W : (k + 1) * W] * (0.0 - flag)

    drain(vpr, f_recv)
    total = vps[p, ylo]
    for n in range(31):
        total = total + vpr[n]
    for g in range(4):
        value = total
        if g:
            value = pltpu.roll(value, 128 - 32 * g, 1)
        v_ref[16 * g : 16 * g + 16, :] = value[:, :32]

    ycopy.wait_send()
    for step in range(8):
        for e in range(2):
            for way in range(2):
                if step < last[way]:
                    ring(way, e, step).wait_send()
    for k in range(KS):
        pair(k).wait_send()
        drain(red.at[k], red_send.at[k])
    drain(vrecv.at[pl.ds(0, 15)], v_send.at[1])

    @pl.when(jnp.logical_not(here))
    def _():
        vpart(0).wait_send()

    for e in range(2):
        home = jnp.logical_and(here, q == 2 * chunk + e)

        @pl.when(jnp.logical_not(home))
        def _():
            ypart(e).wait_send()

    drain(vpr, f_send)


def per_device(sep_inverse, panels, ancestors, window_factor, diag_inverse):
    dma = pltpu.SemaphoreType.DMA
    ys, window = pl.pallas_call(
        kernel,
        out_shape=(
            jax.ShapeDtypeStruct((KS, 2, 8, W), F32),
            jax.ShapeDtypeStruct((64, 32), F32),
        ),
        in_specs=[
            pl.BlockSpec(memory_space=pltpu.VMEM),
            pl.BlockSpec(memory_space=pltpu.VMEM),
            pl.BlockSpec(memory_space=pltpu.SMEM),
            pl.BlockSpec(memory_space=pltpu.VMEM),
            pl.BlockSpec(memory_space=pltpu.VMEM),
        ],
        out_specs=(pl.BlockSpec(memory_space=pltpu.VMEM), pl.BlockSpec(memory_space=pltpu.VMEM)),
        scratch_shapes=[
            pltpu.VMEM((NZ, 2, 16, NC), BF16),
            pltpu.VMEM((NZ, 2, 2, 8, W), F32),
            pltpu.VMEM((W, 512), BF16),
            pltpu.VMEM((KS, 128, W), F32),
            pltpu.VMEM((KS, 128, W), F32),
            pltpu.VMEM((KS, 128, W), F32),
            pltpu.VMEM((KS, 7, 16, W), F32),
            pltpu.VMEM((KS, W, NC), BF16),
            pltpu.VMEM((KS, W, NC), BF16),
            pltpu.VMEM((KS, 512, W), BF16),
            pltpu.VMEM((KS, 512, W), BF16),
            pltpu.VMEM((2, 8, NC), F32),
            pltpu.VMEM((2, 8, NC), F32),
            pltpu.VMEM((NZ, 8, 128), F32),
            pltpu.VMEM((NZ, 8, 128), F32),
            pltpu.VMEM((NZ, 2, 2, 8, 128), F32),
            pltpu.VMEM((8, 32, 128), F32),
            pltpu.VMEM((32, 128), BF16),
            pltpu.VMEM((NP, 2, 16, 128), F32),
            pltpu.VMEM((31, 16, 128), F32),
            dma((2, 2, 8)), dma((2, 2, 8)),
            dma(()), dma(()),
            dma((KS,)), dma((KS,)),
            dma((KS,)), dma((KS,)),
            dma((2,)), dma((2,)),
            dma((2,)), dma(()),
            dma(()), dma(()),
        ],
        compiler_params=pltpu.CompilerParams(collective_id=0, has_side_effects=True),
        name="selinv",
    )(
        sep_inverse.reshape(2, W, W),
        panels.reshape(KS, 2, 8, W),
        ancestors,
        window_factor,
        diag_inverse,
    )
    return ys.reshape(KS, 2, 1, 8, W), window


def solution(mesh):
    placed = (
        P(None, "prow", None, None, "pcol", None),
        P(None, None, "prow", "pcol", None),
        P(),
        P(),
        P(),
    )
    return jax.shard_map(
        per_device,
        mesh=mesh,
        in_specs=placed,
        out_specs=(P(None, None, "prow", "pcol", None), P("prow", "pcol")),
        check_vma=False,
    )
```

```python
import jax
import jax.numpy as jnp
from jax import lax
from jax.experimental import pallas as pl
from jax.experimental.pallas import tpu as pltpu
from jax.sharding import PartitionSpec as P

MESH = pl.DeviceIdType.MESH
F32 = jnp.float32
BF16 = jnp.bfloat16
NP = 16
NZ = 16
W = 256
KS = 4
NC = KS * W


def rem(value, n):
    return lax.rem(value, jnp.int32(n))


def div(value, n):
    return lax.div(value, jnp.int32(n))


def dot(left, right):
    return jnp.dot(left, right, preferred_element_type=F32)


def dot_rows(left, right):
    return lax.dot_general(left, right, (((0,), (0,)), ((), ())), preferred_element_type=F32)


def halves(value):
    high = value.astype(BF16)
    low = (value - high.astype(F32)).astype(BF16)
    return high, low


def pair_index(earlier, later):
    return later * (later - 1) // 2 + earlier


def drain(ref, sem):
    pltpu.make_async_copy(ref, ref, sem).wait()


def kernel(
    s_ref, p_ref, anc_ref, l_ref, d_ref, y_ref, v_ref,
    fg, wide, st, give, keep, pairb, red, mh, ml, uh, ul, ysend, yrecv, vsend, vrecv, wc, dm, dmw, vps, vpr,
    ag_send, ag_recv, ye_send, ye_recv, pair_send, pair_recv, red_send, red_recv,
    y_send, y_recv, v_send, v_recv, f_send, f_recv,
):
    p = lax.axis_index("prow")
    q = lax.axis_index("pcol")
    core = rem(p, 2)
    chip = div(p, 2)
    ylo = div(q, NZ)
    z = rem(q, NZ)

    def copy(src, dst, send, recv, prow, pcol):
        return pltpu.make_async_remote_copy(
            src_ref=src, dst_ref=dst, send_sem=send, recv_sem=recv,
            device_id=(prow, pcol), device_id_type=MESH,
        )

    barrier = pltpu.get_barrier_semaphore()
    greeted = [(p + 1 - 2 * core, q), (p, (1 - ylo) * NZ + z)]
    greeted += [(rem(chip + d, 8) * 2 + core, q) for d in range(1, 8)]
    greeted += [(p, ylo * NZ + rem(z + NZ + a, NZ)) for a in (1, -1, 3, -3, -2)]
    for other in greeted:
        pl.semaphore_signal(barrier, inc=1, device_id=other, device_id_type=MESH)

    for k in range(KS):
        parts = []
        for r in range(2):
            flag = anc_ref[k, r * NP + p].astype(F32)
            parts.append(p_ref[k, r].astype(F32) * flag)
        fg[z, ylo, k] = jnp.concatenate(parts, axis=0).astype(BF16)

    pl.semaphore_wait(barrier, len(greeted))


    def finish(stage):
        if stage >= 1:
            for a in direct:
                hop(0, a).wait_send()
            for a, further in relays.items():
                for b in further:
                    hop(a, b).wait_send()
            for a in range(-7, 9):
                across(a).wait_send()
        if stage >= 2:
            for k in range(KS):
                pair(k).wait_send()
        if stage >= 3:
            for k in range(KS):
                drain(red.at[k], red_send.at[k])
        if stage >= 5:
            drain(vrecv.at[pl.ds(0, 15)], v_send.at[1])

            @pl.when(jnp.logical_not(here))
            def _():
                vpart(0).wait_send()

            for e in range(2):
                home = jnp.logical_and(here, q == 2 * chunk + e)

                @pl.when(jnp.logical_not(home))
                def _():
                    ypart(e).wait_send()
        if stage >= 6:
            drain(vpr, f_send)
        if stage < 6:
            y_ref[...] = jnp.zeros(y_ref.shape, F32)
            v_ref[...] = jnp.zeros(v_ref.shape, F32)

    def hop(a, b):
        at = rem(z + NZ - a, NZ)
        return copy(
            fg.at[at, ylo], fg.at[at, ylo], ag_send.at[a + b + 7], ag_recv.at[a + b + 7],
            p, ylo * NZ + rem(z + NZ + b, NZ),
        )

    def across(a):
        at = rem(z + NZ - a, NZ)
        return copy(
            fg.at[at, ylo], fg.at[at, ylo], ye_send.at[a + 7], ye_recv.at[a + 7], p, (1 - ylo) * NZ + z
        )

    relays = {3: (3, 1, -1), -3: (-3, 1, -1), 6: (2, 1, -1), -6: (-1, 1)}
    direct = (3, -3, 1, -1)

    def task_s(r):
        def run():
            value = s_ref[r].astype(F32).reshape(2, NZ, 8, W)
            for y in range(2):
                wide[:, y, r] = value[y]

        return run

    def task_t():
        st[...] = wide[...].reshape(512, W).T.astype(BF16)

    def put(m, k, value):
        high, low = halves(value)
        mh[m, :, k * W : (k + 1) * W] = high
        ml[m, :, k * W : (k + 1) * W] = low

    def times(m, k, later):
        both = jnp.concatenate(
            [mh[m, :, k * W : (k + 1) * W], ml[m, :, k * W : (k + 1) * W]], axis=0
        )
        out = dot(both, l_ref[pair_index(k, later)])
        return out[:W] + out[W:]

    def coupling(m, k):
        return l_ref[pair_index(m, k)].astype(F32)

    def task_zero():
        rows_at = lax.broadcasted_iota(jnp.int32, (W, W), 0)
        cols_at = lax.broadcasted_iota(jnp.int32, (W, W), 1)
        eye = jnp.where(rows_at == cols_at, 1.0, 0.0).astype(BF16)
        zero = jnp.zeros((W, W), BF16)
        for m in range(KS):
            for k in range(m + 1):
                mh[m, :, k * W : (k + 1) * W] = eye if m == k else zero
                ml[m, :, k * W : (k + 1) * W] = zero
        for m in range(KS - 1):
            put(m, m + 1, -coupling(m, m + 1))

    def task_m2():
        for m in range(2):
            put(m, m + 2, -(coupling(m, m + 2) + times(m, m + 1, m + 2)))

    def task_m3():
        put(0, 3, -(coupling(0, 3) + times(0, 1, 3) + times(0, 2, 3)))

    share = ylo * NP + p
    block = div(share, 8)
    first = pl.multiple_of(rem(share, 8) * 32, 32)
    lane = lax.broadcasted_iota(jnp.int32, (32, 128), 1)

    def task_d():
        dd = d_ref[block, pl.ds(first, 32), :]
        for a in range(8):
            cols = slice(128 * a, 128 * a + 128)
            dm[a] = dot(dd, mh[block, :, cols]) + dot(dd, ml[block, :, cols])
        group = div(z, 4)
        sub = rem(z, 4)
        low_cols = dm[group]
        high_cols = dm[4 + group]
        picked = jnp.zeros((32, 128), F32)
        for b in range(4):
            one = jnp.where(
                lane < 32,
                pltpu.roll(low_cols, (128 - 32 * b) % 128, 1),
                pltpu.roll(high_cols, (160 - 32 * b) % 128, 1),
            )
            picked = jnp.where(sub == b, one, picked)
        picked = jnp.where(lane < 64, picked, 0.0)
        high = picked.astype(BF16).astype(F32)
        dmw[...] = jnp.where(lane < 64, high, pltpu.roll(picked - high, 64, 1)).astype(BF16)

    def task_wc():
        wc[...] = jnp.zeros(wc.shape, F32)

    tasks = [task_s(0), task_s(1), task_t, task_zero, task_m2, task_m3, task_d, task_wc]

    for a in direct:
        hop(0, a).start()
    across(0).start()
    tasks.pop(0)()
    for a in (1, -1, 3, -3, 2, -2, 4, -4, 6, -6, 5, -5, 7, -7, 8):
        hop(0, a).wait_recv()
        for b in relays.get(a, ()):
            hop(a, b).start()
        across(a).start()
        if tasks and a in (1, -1, -2, -4, -6):
            tasks.pop(0)()
    while tasks:
        tasks.pop(0)()
    for a in range(-7, 9):
        across(a).wait_recv()

    def gathered(k):
        return fg[:, :, k].reshape(512, W)

    mine = pl.multiple_of(core * 128, 128)
    theirs = pl.multiple_of((1 - core) * 128, 128)
    mate = p + 1 - 2 * core

    def pair(k):
        return copy(give.at[k], pairb.at[k], pair_send.at[k], pair_recv.at[k], mate, q)

    def spread(k, d):
        to = rem(chip + d, 8)
        rows_to = pl.multiple_of(to * 16, 16)
        return copy(
            keep.at[k, pl.ds(rows_to, 16)], red.at[k, d - 1], red_send.at[k], red_recv.at[k],
            to * 2 + core, q,
        )

    def pass_on(k):
        pair(k).wait_recv()
        keep[k] = keep[k] + pairb[k]
        for d in range(1, 8):
            spread(k, d).start()

    for k in range(KS):
        give[k] = dot(st[pl.ds(theirs, 128), :], gathered(k))
        keep[k] = dot(st[pl.ds(mine, 128), :], gathered(k))
        pair(k).start()
        if k:
            pass_on(k - 1)
    pass_on(KS - 1)
    for k in range(KS):
        if k == 0:
            uh[0] = gathered(0)
            ul[0] = jnp.zeros((512, W), BF16)
        else:
            total = gathered(k).astype(F32)
            for m in range(k):
                left_side = gathered(m)
                cols = slice(k * W, (k + 1) * W)
                total = total + dot(left_side, mh[m, :, cols]) + dot(left_side, ml[m, :, cols])
            high, low = halves(total)
            uh[k] = high
            ul[k] = low

    own_rows = pl.multiple_of(chip * 16, 16)
    blocks = []
    for k in range(KS):
        drain(red.at[k], red_recv.at[k])
        total = keep[k, pl.ds(own_rows, 16), :]
        for d in range(7):
            total = total + red[k, d]
        for m in range(k):
            high, low = halves(blocks[m])
            both = dot(jnp.concatenate([high, low], axis=0), l_ref[pair_index(m, k)])
            total = total - (both[:16] + both[16:])
        blocks.append(total)
        for e in range(2):
            ysend[e, :, k * W : (k + 1) * W] = total[8 * e : 8 * e + 8]

    lane8 = lax.broadcasted_iota(jnp.int32, (8, 128), 1)
    for a in range(4):
        k, at = divmod(128 * a, W)
        first_a = blocks[k][:, at : at + 128]
        second_a = blocks[k + 2][:, at : at + 128]
        for b in range(4):
            def moved(value, group):
                shift = (32 * (group - b)) % 128
                return pltpu.roll(value, shift, 1) if shift else value

            piece = jnp.where(
                lane8 < 64,
                jnp.where(lane8 < 32, moved(first_a[:8], 0), moved(second_a[:8], 1)),
                jnp.where(lane8 < 96, moved(first_a[8:], 2), moved(second_a[8:], 3)),
            )
            vsend[4 * a + b] = piece

    chunk = core * 8 + chip
    here = z == p

    def ypart(e):
        to = 2 * chunk + e
        return copy(ysend.at[e], yrecv.at[ylo], y_send.at[e], y_recv.at[ylo], z, to)

    def ylocal(e):
        return pltpu.make_async_copy(ysend.at[e], yrecv.at[ylo], y_recv.at[ylo])

    def vpart(d):
        to = rem(z + d, NZ)
        return copy(
            vsend.at[to], vrecv.at[chunk], v_send.at[min(d, 1)], v_recv, z, ylo * NZ + to,
        )

    def vlocal():
        return pltpu.make_async_copy(vsend.at[z], vrecv.at[chunk], v_recv)

    for d in range(1, NZ):
        vpart(d).start()

    @pl.when(here)
    def _():
        vlocal().start()

    @pl.when(jnp.logical_not(here))
    def _():
        vpart(0).start()

    for e in range(2):
        home = jnp.logical_and(here, q == 2 * chunk + e)

        @pl.when(home)
        def _():
            ylocal(e).start()

        @pl.when(jnp.logical_not(home))
        def _():
            ypart(e).start()

    drain(vrecv, v_recv)
    got = vrecv[...].reshape(2, 8, 8, 128)
    wide_lane = lax.broadcasted_iota(jnp.int32, (8, 8, 128), 2)
    for y in range(2):
        for h in range(2):
            value = got[y]
            if h:
                value = pltpu.roll(value, 64, 2)
            value = jnp.where(wide_lane < 64, value, 0.0)
            high = value.astype(BF16).astype(F32)
            value = jnp.where(wide_lane < 64, high, pltpu.roll(value - high, 64, 2))
            for n in range(8):
                wc[2 * n + h, y, ylo] = value[n]
    columns = wc[...].reshape(512, 128).astype(BF16)
    lane16 = lax.broadcasted_iota(jnp.int32, (4, 16, 128), 2)
    for k in range(KS):
        cols = slice(k * W, (k + 1) * W)
        total = dot_rows(uh[k], columns) + dot_rows(ul[k], columns)
        total = total + dot_rows(mh[block, pl.ds(first, 32), cols], dmw[...])
        total = total + dot_rows(ml[block, pl.ds(first, 32), cols], dmw[...])
        total = total + pltpu.roll(total, 64, 1)
        total = total.reshape(4, 4, 16, 128)
        for e in range(2):
            packed = None
            for g in range(4):
                shift = (32 * (g - e)) % 128
                value = total[:, g]
                if shift:
                    value = pltpu.roll(value, shift, 2)
                packed = value if packed is None else jnp.where(lane16 < 32 * g, packed, value)
            vps[4 * k : 4 * k + 4, e] = packed

    def final(dp, dy):
        to = rem(p + dp, NP)
        row = rem(ylo + dy, 2)
        return copy(
            vps.at[to, row], vpr.at[2 * dp + dy - 1], f_send, f_recv, to, row * NZ + z
        )

    for dp in range(NP):
        for dy in range(2):
            if dp or dy:
                final(dp, dy).start()

    for r in range(2):
        drain(yrecv.at[r], y_recv.at[r])
        for k in range(KS):
            flag = anc_ref[k, r * NP + p].astype(F32)
            y_ref[k, r] = yrecv[r, :, k * W : (k + 1) * W] * (0.0 - flag)

    drain(vpr, f_recv)
    total = vps[p, ylo]
    for n in range(31):
        total = total + vpr[n]
    for g in range(4):
        value = total
        if g:
            value = pltpu.roll(value, 128 - 32 * g, 1)
        v_ref[16 * g : 16 * g + 16, :] = value[:, :32]

    finish(6)


def per_device(sep_inverse, panels, ancestors, window_factor, diag_inverse):
    dma = pltpu.SemaphoreType.DMA
    ys, window = pl.pallas_call(
        kernel,
        out_shape=(
            jax.ShapeDtypeStruct((KS, 2, 8, W), F32),
            jax.ShapeDtypeStruct((64, 32), F32),
        ),
        in_specs=[
            pl.BlockSpec(memory_space=pltpu.VMEM),
            pl.BlockSpec(memory_space=pltpu.VMEM),
            pl.BlockSpec(memory_space=pltpu.SMEM),
            pl.BlockSpec(memory_space=pltpu.VMEM),
            pl.BlockSpec(memory_space=pltpu.VMEM),
        ],
        out_specs=(pl.BlockSpec(memory_space=pltpu.VMEM), pl.BlockSpec(memory_space=pltpu.VMEM)),
        scratch_shapes=[
            pltpu.VMEM((NZ, 2, KS, 16, W), BF16),
            pltpu.VMEM((NZ, 2, 2, 8, W), F32),
            pltpu.VMEM((W, 512), BF16),
            pltpu.VMEM((KS, 128, W), F32),
            pltpu.VMEM((KS, 128, W), F32),
            pltpu.VMEM((KS, 128, W), F32),
            pltpu.VMEM((KS, 7, 16, W), F32),
            pltpu.VMEM((KS, W, NC), BF16),
            pltpu.VMEM((KS, W, NC), BF16),
            pltpu.VMEM((KS, 512, W), BF16),
            pltpu.VMEM((KS, 512, W), BF16),
            pltpu.VMEM((2, 8, NC), F32),
            pltpu.VMEM((2, 8, NC), F32),
            pltpu.VMEM((NZ, 8, 128), F32),
            pltpu.VMEM((NZ, 8, 128), F32),
            pltpu.VMEM((NZ, 2, 2, 8, 128), F32),
            pltpu.VMEM((8, 32, 128), F32),
            pltpu.VMEM((32, 128), BF16),
            pltpu.VMEM((NP, 2, 16, 128), F32),
            pltpu.VMEM((31, 16, 128), F32),
            dma((16,)), dma((16,)),
            dma((16,)), dma((16,)),
            dma((KS,)), dma((KS,)),
            dma((KS,)), dma((KS,)),
            dma((2,)), dma((2,)),
            dma((2,)), dma(()),
            dma(()), dma(()),
        ],
        compiler_params=pltpu.CompilerParams(collective_id=0, has_side_effects=True),
        name="selinv",
    )(
        sep_inverse.reshape(2, W, W),
        panels.reshape(KS, 2, 8, W),
        ancestors,
        window_factor,
        diag_inverse,
    )
    return ys.reshape(KS, 2, 1, 8, W), window


def solution(mesh):
    placed = (
        P(None, "prow", None, None, "pcol", None),
        P(None, None, "prow", "pcol", None),
        P(),
        P(),
        P(),
    )
    return jax.shard_map(
        per_device,
        mesh=mesh,
        in_specs=placed,
        out_specs=(P(None, None, "prow", "pcol", None), P("prow", "pcol")),
        check_vma=False,
    )
```

```python
import jax
import jax.numpy as jnp
from jax import lax
from jax.experimental import pallas as pl
from jax.experimental.pallas import tpu as pltpu
from jax.sharding import PartitionSpec as P

MESH = pl.DeviceIdType.MESH
F32 = jnp.float32
BF16 = jnp.bfloat16
NP = 16
NZ = 16
W = 256
KS = 4
NC = KS * W


def rem(value, n):
    return lax.rem(value, jnp.int32(n))


def div(value, n):
    return lax.div(value, jnp.int32(n))


def dot(left, right):
    return jnp.dot(left, right, preferred_element_type=F32)


def dot_rows(left, right):
    return lax.dot_general(left, right, (((0,), (0,)), ((), ())), preferred_element_type=F32)


def halves(value):
    high = value.astype(BF16)
    low = (value - high.astype(F32)).astype(BF16)
    return high, low


def pair_index(earlier, later):
    return later * (later - 1) // 2 + earlier


def drain(ref, sem):
    pltpu.make_async_copy(ref, ref, sem).wait()


def kernel(
    s_in, p_in, anc_in, l_in, d_in, y_ref, v_ref,
    s_ref, p_ref, anc_ref, l_ref, d_ref,
    fg, wide, st, give, keep, pairb, red, mh, ml, uh, ul, ysend, yrecv, vsend, vrecv, wc, dm, dmw, dpart, vps, vpr, in_sem,
    ag_send, ag_recv, ye_send, ye_recv, pair_send, pair_recv, red_send, red_recv,
    y_send, y_recv, v_send, v_recv, f_send, f_recv,
):
    p = lax.axis_index("prow")
    q = lax.axis_index("pcol")
    core = rem(p, 2)
    chip = div(p, 2)
    ylo = div(q, NZ)
    z = rem(q, NZ)

    pairs = ((p_in, p_ref), (anc_in, anc_ref), (s_in, s_ref), (l_in, l_ref), (d_in, d_ref))
    fetches = [pltpu.make_async_copy(a, b, in_sem.at[n]) for n, (a, b) in enumerate(pairs)]
    for fetch in fetches:
        fetch.start()

    def copy(src, dst, send, recv, prow, pcol):
        return pltpu.make_async_remote_copy(
            src_ref=src, dst_ref=dst, send_sem=send, recv_sem=recv,
            device_id=(prow, pcol), device_id_type=MESH,
        )

    barrier = pltpu.get_barrier_semaphore()
    greeted = [(p + 1 - 2 * core, q), (p, (1 - ylo) * NZ + z)]
    greeted += [(rem(chip + d, 8) * 2 + core, q) for d in range(1, 8)]
    greeted += [(p, ylo * NZ + rem(z + NZ + a, NZ)) for a in (1, -1, 3, -3, -2)]
    for other in greeted:
        pl.semaphore_signal(barrier, inc=1, device_id=other, device_id_type=MESH)

    fetches[0].wait()
    fetches[1].wait()
    for k in range(KS):
        parts = []
        for r in range(2):
            flag = anc_ref[k, r * NP + p].astype(F32)
            parts.append(p_ref[k, r].astype(F32) * flag)
        fg[ylo, z, k] = jnp.concatenate(parts, axis=0).astype(BF16)

    pl.semaphore_wait(barrier, len(greeted))


    def finish(stage):
        if stage >= 1:
            for a in direct:
                hop(0, a).wait_send()
            for a, further in relays.items():
                for b in further:
                    hop(a, b).wait_send()
            for a in range(-7, 9):
                across(a).wait_send()
        if stage >= 2:
            for k in range(KS):
                pair(k).wait_send()
        if stage >= 3:
            for k in range(KS):
                drain(red.at[k], red_send.at[k])
        if stage >= 5:
            drain(vrecv.at[pl.ds(0, 15)], v_send.at[1])

            @pl.when(jnp.logical_not(here))
            def _():
                vpart(0).wait_send()

            for e in range(2):
                home = jnp.logical_and(here, q == 2 * chunk + e)

                @pl.when(jnp.logical_not(home))
                def _():
                    ypart(e).wait_send()
        if stage >= 6:
            drain(vpr, f_send)
        if stage < 6:
            y_ref[...] = jnp.zeros(y_ref.shape, F32)
            v_ref[...] = jnp.zeros(v_ref.shape, F32)

    def hop(a, b):
        at = rem(z + NZ - a, NZ)
        return copy(
            fg.at[ylo, at], fg.at[ylo, at], ag_send.at[a + b + 7], ag_recv.at[a + b + 7],
            p, ylo * NZ + rem(z + NZ + b, NZ),
        )

    def across(a):
        at = rem(z + NZ - a, NZ)
        return copy(
            fg.at[ylo, at], fg.at[ylo, at], ye_send.at[a + 7], ye_recv.at[a + 7], p, (1 - ylo) * NZ + z
        )

    relays = {3: (3, 1, -1), -3: (-3, 1, -1), 6: (2, 1, -1), -6: (-1, 1)}
    direct = (3, -3, 1, -1)

    def task_s(r):
        def run():
            if r == 0:
                fetches[2].wait()
            value = s_ref[r].astype(F32).reshape(2, NZ, 8, W)
            for y in range(2):
                wide[y, :, r] = value[y]

        return run

    def task_t():
        for y in range(2):
            st[y] = wide[y].reshape(W, W).T.astype(BF16)

    def put(m, k, value):
        high, low = halves(value)
        mh[m, :, k * W : (k + 1) * W] = high
        ml[m, :, k * W : (k + 1) * W] = low

    def times(m, k, later):
        both = jnp.concatenate(
            [mh[m, :, k * W : (k + 1) * W], ml[m, :, k * W : (k + 1) * W]], axis=0
        )
        out = dot(both, l_ref[pair_index(k, later)])
        return out[:W] + out[W:]

    def coupling(m, k):
        return l_ref[pair_index(m, k)].astype(F32)

    def task_zero():
        fetches[3].wait()
        rows_at = lax.broadcasted_iota(jnp.int32, (W, W), 0)
        cols_at = lax.broadcasted_iota(jnp.int32, (W, W), 1)
        eye = jnp.where(rows_at == cols_at, 1.0, 0.0).astype(BF16)
        zero = jnp.zeros((W, W), BF16)
        for m in range(KS):
            for k in range(m + 1):
                mh[m, :, k * W : (k + 1) * W] = eye if m == k else zero
                ml[m, :, k * W : (k + 1) * W] = zero
        for m in range(KS - 1):
            put(m, m + 1, -coupling(m, m + 1))

    def task_m2():
        for m in range(2):
            put(m, m + 2, -(coupling(m, m + 2) + times(m, m + 1, m + 2)))

    def task_m3():
        put(0, 3, -(coupling(0, 3) + times(0, 1, 3) + times(0, 2, 3)))

    share = ylo * NP + p
    block = div(share, 8)
    first = pl.multiple_of(rem(share, 8) * 32, 32)
    lane = lax.broadcasted_iota(jnp.int32, (32, 128), 1)

    def task_d():
        fetches[4].wait()
        dd = d_ref[block, pl.ds(first, 32), :]
        for a in range(8):
            cols = slice(128 * a, 128 * a + 128)
            dm[a] = dot(dd, mh[block, :, cols]) + dot(dd, ml[block, :, cols])
        group = div(z, 4)
        sub = rem(z, 4)
        low_cols = dm[group]
        high_cols = dm[4 + group]
        picked = jnp.zeros((32, 128), F32)
        for b in range(4):
            one = jnp.where(
                lane < 32,
                pltpu.roll(low_cols, (128 - 32 * b) % 128, 1),
                pltpu.roll(high_cols, (160 - 32 * b) % 128, 1),
            )
            picked = jnp.where(sub == b, one, picked)
        picked = jnp.where(lane < 64, picked, 0.0)
        high = picked.astype(BF16).astype(F32)
        dmw[...] = jnp.where(lane < 64, high, pltpu.roll(picked - high, 64, 1)).astype(BF16)
        for k in range(KS):
            cols = slice(k * W, (k + 1) * W)
            dpart[k] = dot_rows(mh[block, pl.ds(first, 32), cols], dmw[...]) + dot_rows(
                ml[block, pl.ds(first, 32), cols], dmw[...]
            )

    tasks = [task_s(0), task_s(1), task_t, task_zero, task_m2, task_m3, task_d]

    for a in direct:
        hop(0, a).start()
    across(0).start()
    tasks.pop(0)()
    for a in (1, -1, 3, -3, 2, -2, 4, -4, 6, -6, 5, -5, 7, -7, 8):
        hop(0, a).wait_recv()
        for b in relays.get(a, ()):
            hop(a, b).start()
        across(a).start()
        if tasks and a in (1, -1, -2, -4, -6):
            tasks.pop(0)()
    mine = pl.multiple_of(core * 128, 128)
    theirs = pl.multiple_of((1 - core) * 128, 128)

    def half(first_row, row, k):
        return dot(st[row, pl.ds(first_row, 128), :], fg[row, :, k].reshape(W, W))

    for k in range(KS):
        give[k] = half(theirs, ylo, k)
        keep[k] = half(mine, ylo, k)
    while tasks:
        tasks.pop(0)()
    for a in range(-7, 9):
        across(a).wait_recv()

    def gathered(k):
        return fg[:, :, k].reshape(512, W)

    mate = p + 1 - 2 * core

    def pair(k):
        return copy(give.at[k], pairb.at[k], pair_send.at[k], pair_recv.at[k], mate, q)

    def slot(at):
        return rem(at + NZ - z, 8)

    def spread(k, d):
        to = rem(chip + d, 8)
        rows_to = pl.multiple_of(slot(to) * 16, 16)
        return copy(
            keep.at[k, pl.ds(rows_to, 16)], red.at[k, d - 1], red_send.at[k], red_recv.at[k],
            to * 2 + core, q,
        )

    def pass_on(k):
        pair(k).wait_recv()
        keep[k] = keep[k] + pairb[k]
        for d in range(1, 8):
            spread(k, d).start()

    for k in range(KS):
        give[k] = give[k] + half(theirs, 1 - ylo, k)
        keep[k] = keep[k] + half(mine, 1 - ylo, k)
        pair(k).start()
        if k:
            pass_on(k - 1)
    pass_on(KS - 1)
    for k in range(KS):
        total = gathered(k).astype(F32)
        for m in range(k):
            left_side = gathered(m)
            cols = slice(k * W, (k + 1) * W)
            total = total + dot(left_side, mh[m, :, cols]) + dot(left_side, ml[m, :, cols])
        wide[...] = total.reshape(2, NZ, 2, 8, W)
        high, low = halves(wide[:, :, ylo].reshape(W, W).T)
        uh[k] = high
        ul[k] = low

    own_rows = pl.multiple_of(slot(chip) * 16, 16)
    blocks = []
    for k in range(KS):
        drain(red.at[k], red_recv.at[k])
        total = keep[k, pl.ds(own_rows, 16), :]
        for d in range(7):
            total = total + red[k, d]
        for m in range(k):
            high, low = halves(blocks[m])
            both = dot(jnp.concatenate([high, low], axis=0), l_ref[pair_index(m, k)])
            total = total - (both[:16] + both[16:])
        blocks.append(total)
        for e in range(2):
            ysend[e, :, k * W : (k + 1) * W] = total[8 * e : 8 * e + 8]

    lane8 = lax.broadcasted_iota(jnp.int32, (8, 128), 1)
    for a in range(4):
        k, at = divmod(128 * a, W)
        first_a = blocks[k][:, at : at + 128]
        second_a = blocks[k + 2][:, at : at + 128]
        for b in range(4):
            def moved(value, group):
                shift = (32 * (group - b)) % 128
                return pltpu.roll(value, shift, 1) if shift else value

            piece = jnp.where(
                lane8 < 64,
                jnp.where(lane8 < 32, moved(first_a[:8], 0), moved(second_a[:8], 1)),
                jnp.where(lane8 < 96, moved(first_a[8:], 2), moved(second_a[8:], 3)),
            )
            vsend[4 * a + b] = piece

    chunk = core * 8 + slot(chip)
    here = z == p

    def ypart(e):
        to = 2 * chunk + e
        return copy(ysend.at[e], yrecv.at[ylo], y_send.at[e], y_recv.at[ylo], z, to)

    def ylocal(e):
        return pltpu.make_async_copy(ysend.at[e], yrecv.at[ylo], y_recv.at[ylo])

    def vpart(d):
        to = rem(z + d, NZ)
        return copy(
            vsend.at[to], vrecv.at[chunk], v_send.at[min(d, 1)], v_recv, z, ylo * NZ + to,
        )

    def vlocal():
        return pltpu.make_async_copy(vsend.at[z], vrecv.at[chunk], v_recv)

    for d in range(1, NZ):
        vpart(d).start()

    @pl.when(here)
    def _():
        vlocal().start()

    @pl.when(jnp.logical_not(here))
    def _():
        vpart(0).start()

    for e in range(2):
        home = jnp.logical_and(here, q == 2 * chunk + e)

        @pl.when(home)
        def _():
            ylocal(e).start()

        @pl.when(jnp.logical_not(home))
        def _():
            ypart(e).start()

    drain(vrecv, v_recv)
    got = vrecv[...].reshape(2, 8, 8, 128)
    wide_lane = lax.broadcasted_iota(jnp.int32, (8, 8, 128), 2)
    for y in range(2):
        for h in range(2):
            value = got[y]
            if h:
                value = pltpu.roll(value, 64, 2)
            value = jnp.where(wide_lane < 64, value, 0.0)
            high = value.astype(BF16).astype(F32)
            value = jnp.where(wide_lane < 64, high, pltpu.roll(value - high, 64, 2))
            for n in range(8):
                wc[y, 2 * n + h] = value[n]
    columns = wc[...].reshape(W, 128).astype(BF16)
    lane16 = lax.broadcasted_iota(jnp.int32, (4, 16, 128), 2)
    for k in range(KS):
        total = dot(uh[k], columns) + dot(ul[k], columns) + dpart[k]
        total = total + pltpu.roll(total, 64, 1)
        total = total.reshape(4, 4, 16, 128)
        for e in range(2):
            packed = None
            for g in range(4):
                shift = (32 * (g - e)) % 128
                value = total[:, g]
                if shift:
                    value = pltpu.roll(value, shift, 2)
                packed = value if packed is None else jnp.where(lane16 < 32 * g, packed, value)
            vps[4 * k : 4 * k + 4, e] = packed

    def final(dp, dy):
        to = rem(p + dp, NP)
        row = rem(ylo + dy, 2)
        return copy(
            vps.at[to, row], vpr.at[2 * dp + dy - 1], f_send, f_recv, to, row * NZ + z
        )

    for dp in range(NP):
        for dy in range(2):
            if dp or dy:
                final(dp, dy).start()

    for r in range(2):
        drain(yrecv.at[r], y_recv.at[r])
        for k in range(KS):
            flag = anc_ref[k, r * NP + p].astype(F32)
            y_ref[k, r] = yrecv[r, :, k * W : (k + 1) * W] * (0.0 - flag)

    drain(vpr, f_recv)
    total = vps[p, ylo]
    for n in range(31):
        total = total + vpr[n]
    parts = [total] + [pltpu.roll(total, 128 - 32 * g, 1) for g in range(1, 4)]
    v_ref[...] = jnp.concatenate(parts, axis=0).T[:32]

    finish(6)


def hand_out(y_in, v_in, y_out, v_out, sem):
    copies = [pltpu.make_async_copy(y_in, y_out, sem.at[0]), pltpu.make_async_copy(v_in, v_out, sem.at[1])]
    for one in copies:
        one.start()
    for one in copies:
        one.wait()


def per_device(sep_inverse, panels, ancestors, window_factor, diag_inverse):
    dma = pltpu.SemaphoreType.DMA
    ys, window = pl.pallas_call(
        kernel,
        out_shape=(
            pltpu.VMEM((KS, 2, 8, W), F32),
            pltpu.VMEM((32, 64), F32),
        ),
        in_specs=[pl.BlockSpec(memory_space=pl.ANY)] * 5,
        out_specs=(pl.BlockSpec(memory_space=pltpu.VMEM), pl.BlockSpec(memory_space=pltpu.VMEM)),
        scratch_shapes=[
            pltpu.VMEM((2, W, W), BF16),
            pltpu.VMEM((KS, 2, 8, W), BF16),
            pltpu.SMEM((KS, 2 * NP), jnp.int32),
            pltpu.VMEM((6, W, W), BF16),
            pltpu.VMEM((KS, W, W), BF16),
            pltpu.VMEM((2, NZ, KS, 16, W), BF16),
            pltpu.VMEM((2, NZ, 2, 8, W), F32),
            pltpu.VMEM((2, W, W), BF16),
            pltpu.VMEM((KS, 128, W), F32),
            pltpu.VMEM((KS, 128, W), F32),
            pltpu.VMEM((KS, 128, W), F32),
            pltpu.VMEM((KS, 7, 16, W), F32),
            pltpu.VMEM((KS, W, NC), BF16),
            pltpu.VMEM((KS, W, NC), BF16),
            pltpu.VMEM((KS, W, W), BF16),
            pltpu.VMEM((KS, W, W), BF16),
            pltpu.VMEM((2, 8, NC), F32),
            pltpu.VMEM((2, 8, NC), F32),
            pltpu.VMEM((NZ, 8, 128), F32),
            pltpu.VMEM((NZ, 8, 128), F32),
            pltpu.VMEM((2, NZ, 8, 128), F32),
            pltpu.VMEM((8, 32, 128), F32),
            pltpu.VMEM((32, 128), BF16),
            pltpu.VMEM((KS, W, 128), F32),
            pltpu.VMEM((NP, 2, 16, 128), F32),
            pltpu.VMEM((31, 16, 128), F32),
            dma((5,)),
            dma((16,)), dma((16,)),
            dma((16,)), dma((16,)),
            dma((KS,)), dma((KS,)),
            dma((KS,)), dma((KS,)),
            dma((2,)), dma((2,)),
            dma((2,)), dma(()),
            dma(()), dma(()),
        ],
        compiler_params=pltpu.CompilerParams(collective_id=0, has_side_effects=True),
        name="selinv",
    )(
        sep_inverse.reshape(2, W, W),
        panels.reshape(KS, 2, 8, W),
        ancestors,
        window_factor,
        diag_inverse,
    )
    vmem = pl.BlockSpec(memory_space=pltpu.VMEM)
    ys, window = pl.pallas_call(
        hand_out,
        out_shape=(
            jax.ShapeDtypeStruct((KS, 2, 8, W), F32),
            jax.ShapeDtypeStruct((32, 64), F32),
        ),
        in_specs=[vmem, vmem],
        out_specs=(pl.BlockSpec(memory_space=pl.ANY),) * 2,
        scratch_shapes=[pltpu.SemaphoreType.DMA((2,))],
        name="hand_out",
    )(
        pltpu.with_memory_space_constraint(ys, pltpu.VMEM),
        pltpu.with_memory_space_constraint(window, pltpu.VMEM),
    )
    return ys.reshape(KS, 2, 1, 8, W), window.T


def solution(mesh):
    placed = (
        P(None, "prow", None, None, "pcol", None),
        P(None, None, "prow", "pcol", None),
        P(),
        P(),
        P(),
    )
    return jax.shard_map(
        per_device,
        mesh=mesh,
        in_specs=placed,
        out_specs=(P(None, None, "prow", "pcol", None), P("prow", "pcol")),
        check_vma=False,
    )
```

```python
import jax
import jax.numpy as jnp
from jax import lax
from jax.experimental import pallas as pl
from jax.experimental.pallas import tpu as pltpu
from jax.sharding import PartitionSpec as P

MESH = pl.DeviceIdType.MESH
F32 = jnp.float32
BF16 = jnp.bfloat16
NP = 16
NZ = 16
W = 256
KS = 4
NC = KS * W


def rem(value, n):
    return lax.rem(value, jnp.int32(n))


def div(value, n):
    return lax.div(value, jnp.int32(n))


def dot(left, right):
    return jnp.dot(left, right, preferred_element_type=F32)


def dot_rows(left, right):
    return lax.dot_general(left, right, (((0,), (0,)), ((), ())), preferred_element_type=F32)


def halves(value):
    high = value.astype(BF16)
    low = (value - high.astype(F32)).astype(BF16)
    return high, low


def pair_index(earlier, later):
    return later * (later - 1) // 2 + earlier


def drain(ref, sem):
    pltpu.make_async_copy(ref, ref, sem).wait()


def kernel(
    s_in, p_in, anc_in, l_in, d_in, y_ref, v_ref,
    s_ref, p_ref, anc_ref, l_ref, d_ref,
    fg, wide, st, give, keep, pairb, red, mh, ml, uh, ul, ysend, yrecv, vsend, vrecv, wc, dm, dmw, dpart, vps, vpr, in_sem,
    ag_send, ag_recv, ye_send, ye_recv, pair_send, pair_recv, red_send, red_recv,
    y_send, y_recv, v_send, v_recv, f_send, f_recv,
):
    p = lax.axis_index("prow")
    q = lax.axis_index("pcol")
    core = rem(p, 2)
    chip = div(p, 2)
    ylo = div(q, NZ)
    z = rem(q, NZ)

    pairs = ((p_in, p_ref), (anc_in, anc_ref), (s_in, s_ref), (l_in, l_ref), (d_in, d_ref))
    fetches = [pltpu.make_async_copy(a, b, in_sem.at[n]) for n, (a, b) in enumerate(pairs)]
    for fetch in fetches:
        fetch.start()

    def copy(src, dst, send, recv, prow, pcol):
        return pltpu.make_async_remote_copy(
            src_ref=src, dst_ref=dst, send_sem=send, recv_sem=recv,
            device_id=(prow, pcol), device_id_type=MESH,
        )

    barrier = pltpu.get_barrier_semaphore()
    greeted = [(p + 1 - 2 * core, q), (p, (1 - ylo) * NZ + z)]
    greeted += [(rem(chip + d, 8) * 2 + core, q) for d in range(1, 8)]
    greeted += [(p, ylo * NZ + rem(z + NZ + a, NZ)) for a in (1, -1, 3, -3, -2)]
    greeted += [(p, (1 - ylo) * NZ + rem(z + NZ + a, NZ)) for a in (1, -1, -2)]
    for other in greeted:
        pl.semaphore_signal(barrier, inc=1, device_id=other, device_id_type=MESH)

    fetches[0].wait()
    fetches[1].wait()
    for k in range(KS):
        parts = []
        for r in range(2):
            flag = anc_ref[k, r * NP + p].astype(F32)
            parts.append(p_ref[k, r].astype(F32) * flag)
        fg[ylo, z, k] = jnp.concatenate(parts, axis=0).astype(BF16)

    pl.semaphore_wait(barrier, len(greeted))


    def finish(stage):
        if stage >= 1:
            for a in direct:
                hop(0, a).wait_send()
            for a, further in relays.items():
                for b in further:
                    hop(a, b).wait_send()
            for a in range(-7, 9):
                across(a).wait_send()
        if stage >= 2:
            for k in range(KS):
                pair(k).wait_send()
        if stage >= 3:
            for k in range(KS):
                drain(red.at[k], red_send.at[k])
        if stage >= 5:
            drain(vrecv.at[pl.ds(0, 15)], v_send.at[1])

            @pl.when(jnp.logical_not(here))
            def _():
                vpart(0).wait_send()

            for e in range(2):
                home = jnp.logical_and(here, q == 2 * chunk + e)

                @pl.when(jnp.logical_not(home))
                def _():
                    ypart(e).wait_send()
        if stage >= 6:
            drain(vpr, f_send)
        if stage < 6:
            y_ref[...] = jnp.zeros(y_ref.shape, F32)
            v_ref[...] = jnp.zeros(v_ref.shape, F32)

    def hop(a, b):
        at = rem(z + NZ - a, NZ)
        return copy(
            fg.at[ylo, at], fg.at[ylo, at], ag_send.at[a + b + 7], ag_recv.at[a + b + 7],
            p, ylo * NZ + rem(z + NZ + b, NZ),
        )

    def slant(a, b):
        at = rem(z + NZ - a, NZ)
        return copy(
            fg.at[ylo, at], fg.at[ylo, at], ye_send.at[a + b + 7], ye_recv.at[a + b + 7],
            p, (1 - ylo) * NZ + rem(z + NZ + b, NZ),
        )

    def across(a):
        at = rem(z + NZ - a, NZ)
        return copy(
            fg.at[ylo, at], fg.at[ylo, at], ye_send.at[a + 7], ye_recv.at[a + 7], p, (1 - ylo) * NZ + z
        )

    relays = {3: (3, 1, -1), -3: (-3, 1, -1), 6: (2, 1, -1), -6: (-1, 1)}
    direct = (3, -3, 1, -1)
    tail = (5, -5, 7, -7, 8)

    def task_s(r):
        def run():
            if r == 0:
                fetches[2].wait()
            value = s_ref[r].astype(F32).reshape(2, NZ, 8, W)
            for y in range(2):
                wide[y, :, r] = value[y]

        return run

    def task_t():
        for y in range(2):
            st[y] = wide[y].reshape(W, W).T.astype(BF16)

    def put(m, k, value):
        high, low = halves(value)
        mh[m, :, k * W : (k + 1) * W] = high
        ml[m, :, k * W : (k + 1) * W] = low

    def times(m, k, later):
        both = jnp.concatenate(
            [mh[m, :, k * W : (k + 1) * W], ml[m, :, k * W : (k + 1) * W]], axis=0
        )
        out = dot(both, l_ref[pair_index(k, later)])
        return out[:W] + out[W:]

    def coupling(m, k):
        return l_ref[pair_index(m, k)].astype(F32)

    def task_zero():
        fetches[3].wait()
        rows_at = lax.broadcasted_iota(jnp.int32, (W, W), 0)
        cols_at = lax.broadcasted_iota(jnp.int32, (W, W), 1)
        eye = jnp.where(rows_at == cols_at, 1.0, 0.0).astype(BF16)
        zero = jnp.zeros((W, W), BF16)
        for m in range(KS):
            for k in range(m + 1):
                mh[m, :, k * W : (k + 1) * W] = eye if m == k else zero
                ml[m, :, k * W : (k + 1) * W] = zero
        for m in range(KS - 1):
            put(m, m + 1, -coupling(m, m + 1))

    def task_m2():
        for m in range(2):
            put(m, m + 2, -(coupling(m, m + 2) + times(m, m + 1, m + 2)))

    def task_m3():
        put(0, 3, -(coupling(0, 3) + times(0, 1, 3) + times(0, 2, 3)))

    share = ylo * NP + p
    block = div(share, 8)
    first = pl.multiple_of(rem(share, 8) * 32, 32)
    lane = lax.broadcasted_iota(jnp.int32, (32, 128), 1)

    def task_d():
        fetches[4].wait()
        dd = d_ref[block, pl.ds(first, 32), :]
        for a in range(8):
            cols = slice(128 * a, 128 * a + 128)
            dm[a] = dot(dd, mh[block, :, cols]) + dot(dd, ml[block, :, cols])
        group = div(z, 4)
        sub = rem(z, 4)
        low_cols = dm[group]
        high_cols = dm[4 + group]
        picked = jnp.zeros((32, 128), F32)
        for b in range(4):
            one = jnp.where(
                lane < 32,
                pltpu.roll(low_cols, (128 - 32 * b) % 128, 1),
                pltpu.roll(high_cols, (160 - 32 * b) % 128, 1),
            )
            picked = jnp.where(sub == b, one, picked)
        picked = jnp.where(lane < 64, picked, 0.0)
        high = picked.astype(BF16).astype(F32)
        dmw[...] = jnp.where(lane < 64, high, pltpu.roll(picked - high, 64, 1)).astype(BF16)
        for k in range(KS):
            cols = slice(k * W, (k + 1) * W)
            dpart[k] = dot_rows(mh[block, pl.ds(first, 32), cols], dmw[...]) + dot_rows(
                ml[block, pl.ds(first, 32), cols], dmw[...]
            )

    tasks = [task_s(0), task_s(1), task_t]

    for a in direct:
        hop(0, a).start()
    across(0).start()
    tasks.pop(0)()
    for a in (1, -1, 3, -3, 2, -2, 4, -4, 6, -6, 5, -5, 7, -7, 8):
        hop(0, a).wait_recv()
        for b in relays.get(a, ()):
            hop(a, b).start()
        if abs(a) == 6:
            for b in relays[a]:
                slant(a, b).start()
        if a not in tail:
            across(a).start()
        if tasks and a in (-3, -6):
            tasks.pop(0)()
    while tasks:
        tasks.pop(0)()
    mine = pl.multiple_of(core * 128, 128)
    theirs = pl.multiple_of((1 - core) * 128, 128)

    def half(first_row, row, k):
        return dot(st[row, pl.ds(first_row, 128), :], fg[row, :, k].reshape(W, W))

    for k in range(KS):
        give[k] = half(theirs, ylo, k)
        keep[k] = half(mine, ylo, k)
    while tasks:
        tasks.pop(0)()
    for a in range(-7, 9):
        across(a).wait_recv()

    def gathered(k):
        return fg[:, :, k].reshape(512, W)

    mate = p + 1 - 2 * core

    def pair(k):
        return copy(give.at[k], pairb.at[k], pair_send.at[k], pair_recv.at[k], mate, q)

    def slot(at):
        return rem(at + NZ - z, 8)

    offsets = ((1, 2), (1, 1), (1, 3), (1, 0), (0, 2), (0, 1), (0, 3))

    def spread(k, d):
        dy, dx = offsets[d - 1]
        to = rem(div(chip, 4) + dy, 2) * 4 + rem(chip + dx, 4)
        rows_to = pl.multiple_of(slot(to) * 16, 16)
        return copy(
            keep.at[k, pl.ds(rows_to, 16)], red.at[k, d - 1], red_send.at[k], red_recv.at[k],
            to * 2 + core, q,
        )

    def pass_on(k):
        pair(k).wait_recv()
        keep[k] = keep[k] + pairb[k]
        for d in range(1, 8):
            spread(k, d).start()

    for k in range(KS):
        give[k] = give[k] + half(theirs, 1 - ylo, k)
        keep[k] = keep[k] + half(mine, 1 - ylo, k)
        pair(k).start()
        if k:
            pass_on(k - 1)
    pass_on(KS - 1)
    task_zero()
    task_m2()
    task_m3()

    own_rows = pl.multiple_of(slot(chip) * 16, 16)
    blocks = []
    for k in range(KS):
        drain(red.at[k], red_recv.at[k])
        total = keep[k, pl.ds(own_rows, 16), :]
        for d in range(7):
            total = total + red[k, d]
        for m in range(k):
            high, low = halves(blocks[m])
            both = dot(jnp.concatenate([high, low], axis=0), l_ref[pair_index(m, k)])
            total = total - (both[:16] + both[16:])
        blocks.append(total)
        for e in range(2):
            ysend[e, :, k * W : (k + 1) * W] = total[8 * e : 8 * e + 8]

    lane8 = lax.broadcasted_iota(jnp.int32, (8, 128), 1)
    for a in range(4):
        k, at = divmod(128 * a, W)
        first_a = blocks[k][:, at : at + 128]
        second_a = blocks[k + 2][:, at : at + 128]
        for b in range(4):
            def moved(value, group):
                shift = (32 * (group - b)) % 128
                return pltpu.roll(value, shift, 1) if shift else value

            piece = jnp.where(
                lane8 < 64,
                jnp.where(lane8 < 32, moved(first_a[:8], 0), moved(second_a[:8], 1)),
                jnp.where(lane8 < 96, moved(first_a[8:], 2), moved(second_a[8:], 3)),
            )
            vsend[4 * a + b] = piece

    chunk = core * 8 + slot(chip)
    here = z == p

    def ypart(e):
        to = 2 * chunk + e
        return copy(ysend.at[e], yrecv.at[ylo], y_send.at[e], y_recv.at[ylo], z, to)

    def ylocal(e):
        return pltpu.make_async_copy(ysend.at[e], yrecv.at[ylo], y_recv.at[ylo])

    def vpart(d):
        to = rem(z + d, NZ)
        return copy(
            vsend.at[to], vrecv.at[chunk], v_send.at[min(d, 1)], v_recv, z, ylo * NZ + to,
        )

    def vlocal():
        return pltpu.make_async_copy(vsend.at[z], vrecv.at[chunk], v_recv)

    for d in (8, 7, 9, 6, 10, 5, 11, 4, 12, 3, 13, 2, 14, 1, 15):
        vpart(d).start()

    @pl.when(here)
    def _():
        vlocal().start()

    @pl.when(jnp.logical_not(here))
    def _():
        vpart(0).start()

    for e in range(2):
        home = jnp.logical_and(here, q == 2 * chunk + e)

        @pl.when(home)
        def _():
            ylocal(e).start()

        @pl.when(jnp.logical_not(home))
        def _():
            ypart(e).start()

    task_d()
    for k in range(KS):
        total = gathered(k).astype(F32)
        for m in range(k):
            left_side = gathered(m)
            cols = slice(k * W, (k + 1) * W)
            total = total + dot(left_side, mh[m, :, cols]) + dot(left_side, ml[m, :, cols])
        wide[...] = total.reshape(2, NZ, 2, 8, W)
        high, low = halves(wide[:, :, ylo].reshape(W, W).T)
        uh[k] = high
        ul[k] = low

    drain(vrecv, v_recv)
    got = vrecv[...].reshape(2, 8, 8, 128)
    wide_lane = lax.broadcasted_iota(jnp.int32, (8, 8, 128), 2)
    for y in range(2):
        for h in range(2):
            value = got[y]
            if h:
                value = pltpu.roll(value, 64, 2)
            value = jnp.where(wide_lane < 64, value, 0.0)
            high = value.astype(BF16).astype(F32)
            value = jnp.where(wide_lane < 64, high, pltpu.roll(value - high, 64, 2))
            for n in range(8):
                wc[y, 2 * n + h] = value[n]
    columns = wc[...].reshape(W, 128).astype(BF16)
    lane16 = lax.broadcasted_iota(jnp.int32, (4, 16, 128), 2)
    for k in range(KS):
        total = dot(uh[k], columns) + dot(ul[k], columns) + dpart[k]
        total = total + pltpu.roll(total, 64, 1)
        total = total.reshape(4, 4, 16, 128)
        for e in range(2):
            packed = None
            for g in range(4):
                shift = (32 * (g - e)) % 128
                value = total[:, g]
                if shift:
                    value = pltpu.roll(value, shift, 2)
                packed = value if packed is None else jnp.where(lane16 < 32 * g, packed, value)
            vps[4 * k : 4 * k + 4, e] = packed

    plane = [
        (dyh, dyl, dx, dc) for dyh in range(2) for dyl in range(2) for dx in range(4) for dc in range(2)
    ]
    plane = sorted(
        plane[1:], key=lambda o: (1 if o[1] else 2 * o[0]) + min(o[2], 4 - o[2]), reverse=True
    )

    def final(n):
        dyh, dyl, dx, dc = plane[n]
        to = rem(div(p, 8) + dyh, 2) * 8 + rem(chip + dx, 4) * 2 + rem(core + dc, 2)
        row = rem(ylo + dyl, 2)
        return copy(vps.at[to, row], vpr.at[n], f_send, f_recv, to, row * NZ + z)

    for n in range(len(plane)):
        final(n).start()

    for r in range(2):
        drain(yrecv.at[r], y_recv.at[r])
        for k in range(KS):
            flag = anc_ref[k, r * NP + p].astype(F32)
            y_ref[k, r] = yrecv[r, :, k * W : (k + 1) * W] * (0.0 - flag)

    drain(vpr, f_recv)
    total = vps[p, ylo]
    for n in range(31):
        total = total + vpr[n]
    parts = [total] + [pltpu.roll(total, 128 - 32 * g, 1) for g in range(1, 4)]
    v_ref[...] = jnp.concatenate(parts, axis=0).T[:32]

    finish(6)


def hand_out(y_in, v_in, y_out, v_out, sem):
    copies = [pltpu.make_async_copy(y_in, y_out, sem.at[0]), pltpu.make_async_copy(v_in, v_out, sem.at[1])]
    for one in copies:
        one.start()
    for one in copies:
        one.wait()


def per_device(sep_inverse, panels, ancestors, window_factor, diag_inverse):
    dma = pltpu.SemaphoreType.DMA
    ys, window = pl.pallas_call(
        kernel,
        out_shape=(
            pltpu.VMEM((KS, 2, 8, W), F32),
            pltpu.VMEM((32, 64), F32),
        ),
        in_specs=[pl.BlockSpec(memory_space=pl.ANY)] * 5,
        out_specs=(pl.BlockSpec(memory_space=pltpu.VMEM), pl.BlockSpec(memory_space=pltpu.VMEM)),
        scratch_shapes=[
            pltpu.VMEM((2, W, W), BF16),
            pltpu.VMEM((KS, 2, 8, W), BF16),
            pltpu.SMEM((KS, 2 * NP), jnp.int32),
            pltpu.VMEM((6, W, W), BF16),
            pltpu.VMEM((KS, W, W), BF16),
            pltpu.VMEM((2, NZ, KS, 16, W), BF16),
            pltpu.VMEM((2, NZ, 2, 8, W), F32),
            pltpu.VMEM((2, W, W), BF16),
            pltpu.VMEM((KS, 128, W), F32),
            pltpu.VMEM((KS, 128, W), F32),
            pltpu.VMEM((KS, 128, W), F32),
            pltpu.VMEM((KS, 7, 16, W), F32),
            pltpu.VMEM((KS, W, NC), BF16),
            pltpu.VMEM((KS, W, NC), BF16),
            pltpu.VMEM((KS, W, W), BF16),
            pltpu.VMEM((KS, W, W), BF16),
            pltpu.VMEM((2, 8, NC), F32),
            pltpu.VMEM((2, 8, NC), F32),
            pltpu.VMEM((NZ, 8, 128), F32),
            pltpu.VMEM((NZ, 8, 128), F32),
            pltpu.VMEM((2, NZ, 8, 128), F32),
            pltpu.VMEM((8, 32, 128), F32),
            pltpu.VMEM((32, 128), BF16),
            pltpu.VMEM((KS, W, 128), F32),
            pltpu.VMEM((NP, 2, 16, 128), F32),
            pltpu.VMEM((31, 16, 128), F32),
            dma((5,)),
            dma((16,)), dma((16,)),
            dma((16,)), dma((16,)),
            dma((KS,)), dma((KS,)),
            dma((KS,)), dma((KS,)),
            dma((2,)), dma((2,)),
            dma((2,)), dma(()),
            dma(()), dma(()),
        ],
        compiler_params=pltpu.CompilerParams(collective_id=0, has_side_effects=True),
        name="selinv",
    )(
        sep_inverse.reshape(2, W, W),
        panels.reshape(KS, 2, 8, W),
        ancestors,
        window_factor,
        diag_inverse,
    )
    vmem = pl.BlockSpec(memory_space=pltpu.VMEM)
    ys, window = pl.pallas_call(
        hand_out,
        out_shape=(
            jax.ShapeDtypeStruct((KS, 2, 8, W), F32),
            jax.ShapeDtypeStruct((32, 64), F32),
        ),
        in_specs=[vmem, vmem],
        out_specs=(pl.BlockSpec(memory_space=pl.ANY),) * 2,
        scratch_shapes=[pltpu.SemaphoreType.DMA((2,))],
        name="hand_out",
    )(
        pltpu.with_memory_space_constraint(ys, pltpu.VMEM),
        pltpu.with_memory_space_constraint(window, pltpu.VMEM),
    )
    return ys.reshape(KS, 2, 1, 8, W), window.T


def solution(mesh):
    placed = (
        P(None, "prow", None, None, "pcol", None),
        P(None, None, "prow", "pcol", None),
        P(),
        P(),
        P(),
    )
    return jax.shard_map(
        per_device,
        mesh=mesh,
        in_specs=placed,
        out_specs=(P(None, None, "prow", "pcol", None), P("prow", "pcol")),
        check_vma=False,
    )
```

```python
import jax
import jax.numpy as jnp
from jax import lax
from jax.experimental import pallas as pl
from jax.experimental.pallas import tpu as pltpu
from jax.sharding import PartitionSpec as P

MESH = pl.DeviceIdType.MESH
F32 = jnp.float32
BF16 = jnp.bfloat16
NP = 16
NZ = 16
W = 256
KS = 4
NC = KS * W


def rem(value, n):
    return lax.rem(value, jnp.int32(n))


def div(value, n):
    return lax.div(value, jnp.int32(n))


def dot(left, right):
    return jnp.dot(left, right, preferred_element_type=F32)


def dot_rows(left, right):
    return lax.dot_general(left, right, (((0,), (0,)), ((), ())), preferred_element_type=F32)


def halves(value):
    high = value.astype(BF16)
    low = (value - high.astype(F32)).astype(BF16)
    return high, low


def pair_index(earlier, later):
    return later * (later - 1) // 2 + earlier


def drain(ref, sem):
    pltpu.make_async_copy(ref, ref, sem).wait()


def kernel(
    s_in, p_in, anc_in, l_in, d_in, y_ref, v_ref,
    s_ref, p_ref, anc_ref, l_ref, d_ref,
    fg, wide, st, give, keep, pairb, red, mh, ml, uh, ul, ysend, yrecv, vsend, vrecv, wc, dm, dmw, dpart, vps, vpr, in_sem,
    ag_send, ag_recv, ye_send, ye_recv, pair_send, pair_recv, red_send, red_recv,
    y_send, y_recv, v_send, v_recv, f_send, f_recv,
):
    p = lax.axis_index("prow")
    q = lax.axis_index("pcol")
    core = rem(p, 2)
    chip = div(p, 2)
    ylo = div(q, NZ)
    z = rem(q, NZ)

    pairs = ((p_in, p_ref), (anc_in, anc_ref), (s_in, s_ref), (l_in, l_ref), (d_in, d_ref))
    fetches = [pltpu.make_async_copy(a, b, in_sem.at[n]) for n, (a, b) in enumerate(pairs)]
    for fetch in fetches:
        fetch.start()

    def copy(src, dst, send, recv, prow, pcol):
        return pltpu.make_async_remote_copy(
            src_ref=src, dst_ref=dst, send_sem=send, recv_sem=recv,
            device_id=(prow, pcol), device_id_type=MESH,
        )

    barrier = pltpu.get_barrier_semaphore()
    greeted = [(p + 1 - 2 * core, q), (p, (1 - ylo) * NZ + z)]
    greeted += [(rem(chip + d, 8) * 2 + core, q) for d in range(1, 8)]
    greeted += [(p, ylo * NZ + rem(z + NZ + a, NZ)) for a in (1, -1, 3, -3, -2)]
    greeted += [(p, (1 - ylo) * NZ + rem(z + NZ + a, NZ)) for a in (1, -1, -2)]
    for other in greeted:
        pl.semaphore_signal(barrier, inc=1, device_id=other, device_id_type=MESH)

    fetches[0].wait()
    fetches[1].wait()
    for k in range(KS):
        parts = []
        for r in range(2):
            flag = anc_ref[k, r * NP + p].astype(F32)
            parts.append(p_ref[k, r].astype(F32) * flag)
        fg[ylo, z, k] = jnp.concatenate(parts, axis=0).astype(BF16)

    pl.semaphore_wait(barrier, len(greeted))


    def finish(stage):
        if stage >= 1:
            for a in direct:
                hop(0, a).wait_send()
            for a, further in relays.items():
                for b in further:
                    hop(a, b).wait_send()
            for a in range(-7, 9):
                across(a).wait_send()
        if stage >= 2:
            for k in range(KS):
                pair(k).wait_send()
        if stage >= 3:
            for k in range(KS):
                drain(red.at[k], red_send.at[k])
        if stage >= 5:
            drain(vrecv.at[pl.ds(0, 15)], v_send.at[1])

            @pl.when(jnp.logical_not(here))
            def _():
                vpart(0).wait_send()

            for e in range(2):
                home = jnp.logical_and(here, q == 2 * chunk + e)

                @pl.when(jnp.logical_not(home))
                def _():
                    ypart(e).wait_send()
        if stage >= 6:
            drain(vpr, f_send)
        if stage < 6:
            y_ref[...] = jnp.zeros(y_ref.shape, F32)
            v_ref[...] = jnp.zeros(v_ref.shape, F32)

    def hop(a, b):
        at = rem(z + NZ - a, NZ)
        return copy(
            fg.at[ylo, at], fg.at[ylo, at], ag_send.at[a + b + 7], ag_recv.at[a + b + 7],
            p, ylo * NZ + rem(z + NZ + b, NZ),
        )

    def slant(a, b):
        at = rem(z + NZ - a, NZ)
        return copy(
            fg.at[ylo, at], fg.at[ylo, at], ye_send.at[a + b + 7], ye_recv.at[a + b + 7],
            p, (1 - ylo) * NZ + rem(z + NZ + b, NZ),
        )

    def across(a):
        at = rem(z + NZ - a, NZ)
        return copy(
            fg.at[ylo, at], fg.at[ylo, at], ye_send.at[a + 7], ye_recv.at[a + 7], p, (1 - ylo) * NZ + z
        )

    relays = {3: (3, 1, -1), -3: (-3, 1, -1), 6: (2, 1, -1), -6: (-1, 1)}
    direct = (3, -3, 1, -1)
    tail = (5, -5, 7, -7, 8)

    def task_s(r):
        def run():
            if r == 0:
                fetches[2].wait()
            value = s_ref[r].astype(F32).reshape(2, NZ, 8, W)
            for y in range(2):
                wide[y, :, r] = value[y]

        return run

    def task_t():
        for y in range(2):
            st[y] = wide[y].reshape(W, W).T.astype(BF16)

    def put(m, k, value):
        high, low = halves(value)
        mh[m, :, k * W : (k + 1) * W] = high
        ml[m, :, k * W : (k + 1) * W] = low

    def times(m, k, later):
        both = jnp.concatenate(
            [mh[m, :, k * W : (k + 1) * W], ml[m, :, k * W : (k + 1) * W]], axis=0
        )
        out = dot(both, l_ref[pair_index(k, later)])
        return out[:W] + out[W:]

    def coupling(m, k):
        return l_ref[pair_index(m, k)].astype(F32)

    def task_zero():
        fetches[3].wait()
        rows_at = lax.broadcasted_iota(jnp.int32, (W, W), 0)
        cols_at = lax.broadcasted_iota(jnp.int32, (W, W), 1)
        eye = jnp.where(rows_at == cols_at, 1.0, 0.0).astype(BF16)
        zero = jnp.zeros((W, W), BF16)
        for m in range(KS):
            for k in range(m + 1):
                mh[m, :, k * W : (k + 1) * W] = eye if m == k else zero
                ml[m, :, k * W : (k + 1) * W] = zero
        for m in range(KS - 1):
            put(m, m + 1, -coupling(m, m + 1))

    def task_m2():
        for m in range(2):
            put(m, m + 2, -(coupling(m, m + 2) + times(m, m + 1, m + 2)))

    def task_m3():
        put(0, 3, -(coupling(0, 3) + times(0, 1, 3) + times(0, 2, 3)))

    share = ylo * NP + p
    block = div(share, 8)
    first = pl.multiple_of(rem(share, 8) * 32, 32)
    lane = lax.broadcasted_iota(jnp.int32, (32, 128), 1)

    def task_d():
        fetches[4].wait()
        dd = d_ref[block, pl.ds(first, 32), :]
        for a in range(8):
            cols = slice(128 * a, 128 * a + 128)
            dm[a] = dot(dd, mh[block, :, cols]) + dot(dd, ml[block, :, cols])
        group = div(z, 4)
        sub = rem(z, 4)
        low_cols = dm[group]
        high_cols = dm[4 + group]
        picked = jnp.zeros((32, 128), F32)
        for b in range(4):
            one = jnp.where(
                lane < 32,
                pltpu.roll(low_cols, (128 - 32 * b) % 128, 1),
                pltpu.roll(high_cols, (160 - 32 * b) % 128, 1),
            )
            picked = jnp.where(sub == b, one, picked)
        picked = jnp.where(lane < 64, picked, 0.0)
        high = picked.astype(BF16).astype(F32)
        dmw[...] = jnp.where(lane < 64, high, pltpu.roll(picked - high, 64, 1)).astype(BF16)
        for k in range(KS):
            cols = slice(k * W, (k + 1) * W)
            dpart[k] = dot_rows(mh[block, pl.ds(first, 32), cols], dmw[...]) + dot_rows(
                ml[block, pl.ds(first, 32), cols], dmw[...]
            )

    tasks = [task_s(0), task_s(1), task_t]

    for a in direct:
        hop(0, a).start()
    across(0).start()
    tasks.pop(0)()
    for a in (1, -1, 3, -3, 6, -6, 2, -2, 4, -4, 5, -5, 7, -7, 8):
        hop(0, a).wait_recv()
        for b in relays.get(a, ()):
            hop(a, b).start()
        if abs(a) == 6:
            for b in relays[a]:
                slant(a, b).start()
        if a not in tail:
            across(a).start()
        if tasks and a in (-3, -6):
            tasks.pop(0)()
    while tasks:
        tasks.pop(0)()
    mine = pl.multiple_of(core * 128, 128)
    theirs = pl.multiple_of((1 - core) * 128, 128)

    def half(first_row, row, k):
        return dot(st[row, pl.ds(first_row, 128), :], fg[row, :, k].reshape(W, W))

    for k in range(KS):
        give[k] = half(theirs, ylo, k)
        keep[k] = half(mine, ylo, k)
    while tasks:
        tasks.pop(0)()
    for a in range(-7, 9):
        across(a).wait_recv()

    def gathered(k):
        return fg[:, :, k].reshape(512, W)

    mate = p + 1 - 2 * core

    def pair(k):
        return copy(give.at[k], pairb.at[k], pair_send.at[k], pair_recv.at[k], mate, q)

    def slot(at):
        return rem(at + NZ - z, 8)

    offsets = ((1, 2), (1, 1), (1, 3), (1, 0), (0, 2), (0, 1), (0, 3))

    def spread(k, d):
        dy, dx = offsets[d - 1]
        to = rem(div(chip, 4) + dy, 2) * 4 + rem(chip + dx, 4)
        rows_to = pl.multiple_of(slot(to) * 16, 16)
        return copy(
            keep.at[k, pl.ds(rows_to, 16)], red.at[k, d - 1], red_send.at[k], red_recv.at[k],
            to * 2 + core, q,
        )

    def pass_on(k):
        pair(k).wait_recv()
        keep[k] = keep[k] + pairb[k]
        for d in range(1, 8):
            spread(k, d).start()

    for k in range(KS):
        give[k] = give[k] + half(theirs, 1 - ylo, k)
        keep[k] = keep[k] + half(mine, 1 - ylo, k)
        pair(k).start()
        if k:
            pass_on(k - 1)
    pass_on(KS - 1)
    task_zero()
    task_m2()
    task_m3()

    own_rows = pl.multiple_of(slot(chip) * 16, 16)
    blocks = []
    for k in range(KS):
        drain(red.at[k], red_recv.at[k])
        total = keep[k, pl.ds(own_rows, 16), :]
        for d in range(7):
            total = total + red[k, d]
        for m in range(k):
            high, low = halves(blocks[m])
            both = dot(jnp.concatenate([high, low], axis=0), l_ref[pair_index(m, k)])
            total = total - (both[:16] + both[16:])
        blocks.append(total)
        for e in range(2):
            ysend[e, :, k * W : (k + 1) * W] = total[8 * e : 8 * e + 8]

    lane8 = lax.broadcasted_iota(jnp.int32, (8, 128), 1)
    for a in range(4):
        k, at = divmod(128 * a, W)
        first_a = blocks[k][:, at : at + 128]
        second_a = blocks[k + 2][:, at : at + 128]
        for b in range(4):
            def moved(value, group):
                shift = (32 * (group - b)) % 128
                return pltpu.roll(value, shift, 1) if shift else value

            piece = jnp.where(
                lane8 < 64,
                jnp.where(lane8 < 32, moved(first_a[:8], 0), moved(second_a[:8], 1)),
                jnp.where(lane8 < 96, moved(first_a[8:], 2), moved(second_a[8:], 3)),
            )
            vsend[4 * a + b] = piece

    chunk = core * 8 + slot(chip)
    here = z == p

    def ypart(e):
        to = 2 * chunk + e
        return copy(ysend.at[e], yrecv.at[ylo], y_send.at[e], y_recv.at[ylo], z, to)

    def ylocal(e):
        return pltpu.make_async_copy(ysend.at[e], yrecv.at[ylo], y_recv.at[ylo])

    def vpart(d):
        to = rem(z + d, NZ)
        return copy(
            vsend.at[to], vrecv.at[chunk], v_send.at[min(d, 1)], v_recv, z, ylo * NZ + to,
        )

    def vlocal():
        return pltpu.make_async_copy(vsend.at[z], vrecv.at[chunk], v_recv)

    for d in (8, 7, 9, 6, 10, 5, 11, 4, 12, 3, 13, 2, 14, 1, 15):
        vpart(d).start()

    @pl.when(here)
    def _():
        vlocal().start()

    @pl.when(jnp.logical_not(here))
    def _():
        vpart(0).start()

    for e in range(2):
        home = jnp.logical_and(here, q == 2 * chunk + e)

        @pl.when(home)
        def _():
            ylocal(e).start()

        @pl.when(jnp.logical_not(home))
        def _():
            ypart(e).start()

    task_d()
    for k in range(KS):
        total = gathered(k).astype(F32)
        for m in range(k):
            left_side = gathered(m)
            cols = slice(k * W, (k + 1) * W)
            total = total + dot(left_side, mh[m, :, cols]) + dot(left_side, ml[m, :, cols])
        wide[...] = total.reshape(2, NZ, 2, 8, W)
        high, low = halves(wide[:, :, ylo].reshape(W, W).T)
        uh[k] = high
        ul[k] = low

    drain(vrecv, v_recv)
    got = vrecv[...].reshape(2, 8, 8, 128)
    wide_lane = lax.broadcasted_iota(jnp.int32, (8, 8, 128), 2)
    for y in range(2):
        for h in range(2):
            value = got[y]
            if h:
                value = pltpu.roll(value, 64, 2)
            value = jnp.where(wide_lane < 64, value, 0.0)
            high = value.astype(BF16).astype(F32)
            value = jnp.where(wide_lane < 64, high, pltpu.roll(value - high, 64, 2))
            for n in range(8):
                wc[y, 2 * n + h] = value[n]
    columns = wc[...].reshape(W, 128).astype(BF16)
    lane16 = lax.broadcasted_iota(jnp.int32, (4, 16, 128), 2)
    for k in range(KS):
        total = dot(uh[k], columns) + dot(ul[k], columns) + dpart[k]
        total = total + pltpu.roll(total, 64, 1)
        total = total.reshape(4, 4, 16, 128)
        for e in range(2):
            packed = None
            for g in range(4):
                shift = (32 * (g - e)) % 128
                value = total[:, g]
                if shift:
                    value = pltpu.roll(value, shift, 2)
                packed = value if packed is None else jnp.where(lane16 < 32 * g, packed, value)
            vps[4 * k : 4 * k + 4, e] = packed

    plane = [
        (dyh, dyl, dx, dc) for dyh in range(2) for dyl in range(2) for dx in range(4) for dc in range(2)
    ]
    plane = sorted(
        plane[1:], key=lambda o: (1 if o[1] else 2 * o[0]) + min(o[2], 4 - o[2]), reverse=True
    )

    def final(n):
        dyh, dyl, dx, dc = plane[n]
        to = rem(div(p, 8) + dyh, 2) * 8 + rem(chip + dx, 4) * 2 + rem(core + dc, 2)
        row = rem(ylo + dyl, 2)
        return copy(vps.at[to, row], vpr.at[n], f_send, f_recv, to, row * NZ + z)

    for n in range(len(plane)):
        final(n).start()

    for r in range(2):
        drain(yrecv.at[r], y_recv.at[r])
        for k in range(KS):
            flag = anc_ref[k, r * NP + p].astype(F32)
            y_ref[k, r] = yrecv[r, :, k * W : (k + 1) * W] * (0.0 - flag)

    drain(vpr, f_recv)
    total = vps[p, ylo]
    for n in range(31):
        total = total + vpr[n]
    parts = [total] + [pltpu.roll(total, 128 - 32 * g, 1) for g in range(1, 4)]
    v_ref[...] = jnp.concatenate(parts, axis=0).T[:32]

    finish(6)


def hand_out(y_in, v_in, y_out, v_out, sem):
    copies = [pltpu.make_async_copy(y_in, y_out, sem.at[0]), pltpu.make_async_copy(v_in, v_out, sem.at[1])]
    for one in copies:
        one.start()
    for one in copies:
        one.wait()


def per_device(sep_inverse, panels, ancestors, window_factor, diag_inverse):
    dma = pltpu.SemaphoreType.DMA
    ys, window = pl.pallas_call(
        kernel,
        out_shape=(
            pltpu.VMEM((KS, 2, 8, W), F32),
            pltpu.VMEM((32, 64), F32),
        ),
        in_specs=[pl.BlockSpec(memory_space=pl.ANY)] * 5,
        out_specs=(pl.BlockSpec(memory_space=pltpu.VMEM), pl.BlockSpec(memory_space=pltpu.VMEM)),
        scratch_shapes=[
            pltpu.VMEM((2, W, W), BF16),
            pltpu.VMEM((KS, 2, 8, W), BF16),
            pltpu.SMEM((KS, 2 * NP), jnp.int32),
            pltpu.VMEM((6, W, W), BF16),
            pltpu.VMEM((KS, W, W), BF16),
            pltpu.VMEM((2, NZ, KS, 16, W), BF16),
            pltpu.VMEM((2, NZ, 2, 8, W), F32),
            pltpu.VMEM((2, W, W), BF16),
            pltpu.VMEM((KS, 128, W), F32),
            pltpu.VMEM((KS, 128, W), F32),
            pltpu.VMEM((KS, 128, W), F32),
            pltpu.VMEM((KS, 7, 16, W), F32),
            pltpu.VMEM((KS, W, NC), BF16),
            pltpu.VMEM((KS, W, NC), BF16),
            pltpu.VMEM((KS, W, W), BF16),
            pltpu.VMEM((KS, W, W), BF16),
            pltpu.VMEM((2, 8, NC), F32),
            pltpu.VMEM((2, 8, NC), F32),
            pltpu.VMEM((NZ, 8, 128), F32),
            pltpu.VMEM((NZ, 8, 128), F32),
            pltpu.VMEM((2, NZ, 8, 128), F32),
            pltpu.VMEM((8, 32, 128), F32),
            pltpu.VMEM((32, 128), BF16),
            pltpu.VMEM((KS, W, 128), F32),
            pltpu.VMEM((NP, 2, 16, 128), F32),
            pltpu.VMEM((31, 16, 128), F32),
            dma((5,)),
            dma((16,)), dma((16,)),
            dma((16,)), dma((16,)),
            dma((KS,)), dma((KS,)),
            dma((KS,)), dma((KS,)),
            dma((2,)), dma((2,)),
            dma((2,)), dma(()),
            dma(()), dma(()),
        ],
        compiler_params=pltpu.CompilerParams(collective_id=0, has_side_effects=True),
        name="selinv",
    )(
        sep_inverse.reshape(2, W, W),
        panels.reshape(KS, 2, 8, W),
        ancestors,
        window_factor,
        diag_inverse,
    )
    vmem = pl.BlockSpec(memory_space=pltpu.VMEM)
    ys, window = pl.pallas_call(
        hand_out,
        out_shape=(
            jax.ShapeDtypeStruct((KS, 2, 8, W), F32),
            jax.ShapeDtypeStruct((32, 64), F32),
        ),
        in_specs=[vmem, vmem],
        out_specs=(pl.BlockSpec(memory_space=pl.ANY),) * 2,
        scratch_shapes=[pltpu.SemaphoreType.DMA((2,))],
        name="hand_out",
    )(
        pltpu.with_memory_space_constraint(ys, pltpu.VMEM),
        pltpu.with_memory_space_constraint(window, pltpu.VMEM),
    )
    return ys.reshape(KS, 2, 1, 8, W), window.T


def solution(mesh):
    placed = (
        P(None, "prow", None, None, "pcol", None),
        P(None, None, "prow", "pcol", None),
        P(),
        P(),
        P(),
    )
    return jax.shard_map(
        per_device,
        mesh=mesh,
        in_specs=placed,
        out_specs=(P(None, None, "prow", "pcol", None), P("prow", "pcol")),
        check_vma=False,
    )
```
